32 devices in a mesh: groups: 2 (over y), slab: 4 (over z), chan: 4 (over x, core).
Axes of the slice: x: 2, y: 2, z: 4, core: 2. Of those that a mesh axis runs over, the one named last changes fastest.
Arguments:
- field: float32 [64, 8, 512], P('chan', ('groups', 'slab')), parts along dimension 1, may hold values from -6 to 6
- order: int32 [2, 64], replicated, may hold values from 0 to 63, each once within a row
- w_first: bfloat16 [2, 512, 864], P(None, 'chan'), may hold values from -0.21875 to 0.21875
- b_first: bfloat16 [2, 512], P(None, 'chan'), may hold values from -3 to 3
- w_middle: bfloat16 [2, 512, 512], P(None, 'chan'), may hold values from -0.375 to 0.375
- b_middle: bfloat16 [2, 512], P(None, 'chan'), may hold values from -3 to 3
- w_last: bfloat16 [2, 1728, 512], P(None, None, 'chan'), may hold values from -0.078125 to 0.078125
- b_last: bfloat16 [2, 64], replicated, may hold values from -3 to 3
Outputs:
- flowed: float32 [64, 8, 512], P('chan', ('groups', 'slab')), parts along dimension 1
- logscale: float32 [2, 32, 8], P(None, 'chan', ('groups', 'slab')), parts along dimension 2
The draws below stay inside these ranges and needn't reach their ends.
There are 2 independent parts, one for each index of `groups`. The reference program is written for one: setup_inputs(seed, part) draws one part's arguments, and reference() takes and returns one part's arrays. A program takes and returns all parts, laid end to end along the dimension named above; an argument that names none is the same for every part. Nothing has to cross between parts.
Inputs may be any that keep to these rules, and one draw needn't show every extreme that they name: Each row of order names every channel once.
All inputs are finite; a program needn't handle non-finite values.
Results may differ from the reference program's by a relative error of at most 0.0095.
Values may be sent and summed in bfloat16 or wider, within the bound.
A program may use at most 64 MiB of HBM per device.

```python
import jax
import jax.numpy as jnp
from jax import lax

C = 64
HID = 512
STEPS = 2
NX = 8
NY = 64
NZ = 4
NXY = 512
HALF = 32
K1 = 864
K3 = 1728


def levels(stream_key, shape, shards, least, largest):
    factor_of = 1.0
    for position, blocks in shards:
        draws = jax.random.uniform(jax.random.fold_in(jax.random.fold_in(stream_key, 6), position), (blocks,), jnp.float32, least / len(shards), largest / len(shards))
        factor_of = factor_of * jnp.repeat(jnp.exp(draws), shape[position] // blocks).reshape((-1,) + (1,) * (len(shape) - 1 - position))
    return factor_of


def bell_draw(rng, dims, width, reach, pieces=(), dtype=jnp.bfloat16):
    values = width * jax.random.normal(rng, dims, jnp.float32)
    if pieces:
        values = values * levels(rng, dims, pieces, -0.22, 0.18)
    return jnp.clip(values, -reach, reach).astype(dtype)


def setup_inputs(seed: int = 0, part: int = 0) -> dict:
    key_list = jax.random.split(jax.random.key(seed), 9)
    part_keys = jax.random.split(jax.random.fold_in(key_list[8], part), 9)
    return {
        "field": bell_draw(part_keys[0], (C, NZ, NXY), 1.0, 6.0, ((0, 4), (1, 4)), jnp.float32),
        "order": jax.vmap(lambda own: jax.random.permutation(own, C))(jax.random.split(key_list[1], STEPS)).reshape((STEPS, C)).astype(jnp.int32),
        "w_first": bell_draw(key_list[2], (STEPS, HID, K1), K1 ** -0.5, 0.21875, ((1, 4),)),
        "b_first": bell_draw(key_list[3], (STEPS, HID), 0.5, 3.0, ((1, 4),)),
        "w_middle": bell_draw(key_list[4], (STEPS, HID, HID), (HID // 2) ** -0.5, 0.375, ((1, 4),)),
        "b_middle": bell_draw(key_list[5], (STEPS, HID), 0.5, 3.0, ((1, 4),)),
        "w_last": bell_draw(key_list[6], (STEPS, K3, HID), (HID * 27 // 2) ** -0.5, 0.078125, ((2, 4),)),
        "b_last": bell_draw(key_list[7], (STEPS, C), 0.5, 3.0),
    }


def conv_same(inputs, kernel):
    result = lax.conv_general_dilated(inputs[None], kernel, (1, 1, 1), ((1, 1), (1, 1), (1, 1)), dimension_numbers=("NCDHW", "OIDHW", "NCDHW"), precision=lax.Precision.HIGHEST)
    return result[0]


def reference(field, order, w_first, b_first, w_middle, b_middle, w_last, b_last):
    current = field
    records = []
    for section in range(STEPS):
        permuted = jnp.take(current, order[section], axis=0)
        front = permuted[:HALF]
        back = permuted[HALF:]
        front_bf = lax.optimization_barrier(front.astype(jnp.bfloat16))
        grid_in = front_bf.astype(jnp.float32).reshape(HALF, NZ, NX, NY)
        kernel_one = w_first[section].astype(jnp.float32).reshape(HID, 3, 3, 3, HALF).transpose(0, 4, 1, 2, 3)
        hidden_one = jax.nn.relu(conv_same(grid_in, kernel_one) + b_first[section].astype(jnp.float32)[:, None, None, None])
        hidden_one = hidden_one.astype(jnp.bfloat16).reshape(HID, NZ * NXY)
        middle = jnp.dot(w_middle[section], hidden_one, preferred_element_type=jnp.float32)
        hidden_two = jax.nn.relu(middle + b_middle[section].astype(jnp.float32)[:, None]).astype(jnp.bfloat16)
        kernel_three = w_last[section].astype(jnp.float32).reshape(3, 3, 3, C, HID).transpose(3, 4, 0, 1, 2)
        net = conv_same(hidden_two.astype(jnp.float32).reshape(HID, NZ, NX, NY), kernel_three)
        net = net.reshape(C, NZ, NXY) + b_last[section].astype(jnp.float32)[:, None, None]
        shifted = net[:HALF] + 2.0
        scale = jax.nn.sigmoid(shifted)
        coupled = (back + net[HALF:]) * scale
        records.append(jnp.mean(jax.nn.log_sigmoid(shifted), axis=2))
        current = jnp.concatenate([front, coupled], axis=0)
    return current, jnp.stack(records)
```

```python
import jax
import jax.numpy as jnp
from jax import lax
from jax.experimental import pallas as pl
from jax.experimental.pallas import tpu as pltpu
from jax.sharding import PartitionSpec as P

C = 64
HALF = 32
STEPS = 2
NY = 64
NXY = 512
PAD = 128
CHUNKS = 3
SEMS = 80
MESH = pl.DeviceIdType.MESH
F32 = jnp.float32
BF16 = jnp.bfloat16


def kernel(
    field, order, w_first, b_first, w_middle, b_middle, w_last, b_last,
    flowed, logscale,
    field_in, wf, wm, wl, bias2, bias3, perm,
    whole, xpad, patches, hidden, hpad, patches3, psend, precv,
    back, csend, cgot, fronts, final_send, final,
    load_sem, send_sem, recv_sem, out_sem,
):
    n_chan = lax.axis_size("chan")
    assert n_chan == 4
    n_slab = lax.axis_size("slab")
    c = lax.axis_index("chan")
    z = lax.axis_index("slab")
    share = HALF // n_chan
    own = C // n_chan
    units = wf.shape[3]
    cuts = [slice(0, 9 * HALF), slice(9 * HALF, 18 * HALF), slice(18 * HALF, 27 * HALF + 16)]
    has = {0: z > 0, 1: None, 2: z < n_slab - 1}

    place_of = (c, c + 1 - 2 * lax.rem(c, 2), lax.rem(c + 2, 4), 3 - c)
    slots = {}

    def slot(*key):
        index = slots.setdefault(key, len(slots))
        assert index < SEMS
        return index

    def peer(dz, j):
        return {"slab": z + dz, "chan": place_of[j]}

    def when_side(dz, fn):
        if dz == 0:
            fn()
        elif dz < 0:
            pl.when(z > 0)(fn)
        else:
            pl.when(z < n_slab - 1)(fn)

    def each_peer(fn):
        for j in (2, 3, 1):
            fn(0, j)
        for dz in (-1, 1):
            when_side(dz, lambda dz=dz: [fn(dz, j) for j in range(n_chan)] and None)

    loads = [pltpu.make_async_copy(field.at[:, 0, :], field_in, load_sem.at[0])]
    for k in range(STEPS):
        taps = wf.at[k, c, 0 : 27 * HALF, :]
        loads.append(pltpu.make_async_copy(w_first.at[k], taps, load_sem.at[1 + k]))
    loads.append(pltpu.make_async_copy(w_middle, wm, load_sem.at[3]))
    n = 4
    for k in range(STEPS):
        for a in range(3):
            loads.append(
                pltpu.make_async_copy(
                    w_last.at[k, a], wl.at[k, :, pl.ds(a * C, C), :], load_sem.at[n]
                )
            )
            n += 1
    for load in loads:
        load.start()

    barrier = pltpu.get_barrier_semaphore()

    def greet(dz, j):
        pl.semaphore_signal(barrier, inc=1, device_id=peer(dz, j), device_id_type=MESH)

    each_peer(greet)

    line = lax.broadcasted_iota(jnp.int32, (C, C), 0)
    block = lax.div(line, own)
    channel = (2 * lax.rem(block, 2) + lax.div(block, 2)) * own + lax.rem(line, own)
    for k in range(STEPS):
        row = order[k : k + 1, :]
        hit = ((channel if k == 0 else line) == row).astype(F32)
        perm[k] = hit.T.astype(BF16)
        lone = lax.broadcasted_iota(jnp.int32, (16, units), 0) == 0
        wf[k, c, 27 * HALF :, :] = jnp.where(lone, b_first[k : k + 1, :].astype(F32), 0.0).astype(BF16)
        bias2[k] = jnp.broadcast_to(b_middle[k : k + 1, :].astype(F32), (128, units)).T
        bias3[k] = jnp.broadcast_to(b_last[k : k + 1, :].astype(F32), (128, C)).T
    for e in range(3):
        xpad[e, :, 0:PAD] = jnp.zeros((3 * HALF, PAD), BF16)
        xpad[e, :, PAD + NXY :] = jnp.zeros((3 * HALF, PAD), BF16)
        hpad[e, :, 0:PAD] = jnp.zeros((units, PAD), BF16)
        hpad[e, :, PAD + NXY :] = jnp.zeros((units, PAD), BF16)
    patches[27 * HALF :, :] = jnp.ones((16, NXY), BF16)
    for a in (0, 2):

        @pl.when(jnp.logical_not(has[a]))
        def _():
            whole[a] = jnp.zeros((C, NXY), BF16)
            cgot[a] = jnp.zeros((n_chan, 2 * share, NXY // 2), BF16)
            for k in range(STEPS):
                precv[k, a] = jnp.zeros((n_chan, 2 * share, NXY), BF16)

    def rows_of(place):
        at = 2 * lax.rem(place, 2) + lax.div(place, 2)
        return pl.ds(pl.multiple_of(at * own, own), own)

    mine = rows_of(c)
    theirs = rows_of(place_of[2])
    pair = pl.ds(pl.multiple_of(lax.rem(c, 2) * 2 * own, 2 * own), 2 * own)
    other_pair = pl.ds(pl.multiple_of((1 - lax.rem(c, 2)) * 2 * own, 2 * own), 2 * own)
    loads[0].wait()
    whole[1, mine, :] = field_in[...].astype(BF16)

    sides = jnp.where(z > 0, 1, 0) + jnp.where(z < n_slab - 1, 1, 0)
    pl.semaphore_wait(barrier, n_chan - 1 + n_chan * sides)

    def copy(tag, dz, j, src, dst):
        i = slot(tag, dz, j)
        return pltpu.make_async_remote_copy(
            src_ref=src,
            dst_ref=dst,
            send_sem=send_sem.at[i],
            recv_sem=recv_sem.at[i],
            device_id=peer(dz, j),
            device_id_type=MESH,
        )

    def arrive(tag, dz, j, dst):
        i = slot(tag, dz, j)
        pltpu.make_async_remote_copy(
            src_ref=dst,
            dst_ref=dst,
            send_sem=send_sem.at[i],
            recv_sem=recv_sem.at[i],
            device_id=peer(0, 1),
            device_id_type=MESH,
        ).wait_recv()

    def field_copy(dz, j):
        return copy("field", dz, j, whole.at[1, mine, :], whole.at[1 - dz, mine, :])

    field_to = ((-1, 2), (1, 2), (0, 2), (-1, 0), (1, 0), (0, 1))
    for dz, j in field_to:
        when_side(dz, lambda dz=dz, j=j: field_copy(dz, j).start())

    def first_copy(k, i, j):
        part = cuts[i]
        return copy(("first", k, i), 0, j, wf.at[k, c, part, :], wf.at[k, c, part, :])

    def first_relay(k, i):
        part = wf.at[k, place_of[2], cuts[i], :]
        return copy(("first relay", k, i), 0, 1, part, part)

    def first_arrives(k, i):
        arrive(("first", k, i), 0, 2, wf.at[k, place_of[2], cuts[i], :])

    loads[1].wait()
    for i in range(CHUNKS):
        first_copy(0, i, 2).start()
    for i in range(CHUNKS):
        first_copy(0, i, 1).start()

    def field_relay(a):
        part = whole.at[a, theirs if a == 1 else pair, :]
        return copy(("field relay", a), 0, 1, part, part)

    def on_side(a, fn):
        when_side(a - 1, fn)

    def from_columns(a):
        if a != 1:
            arrive("field", 1 - a, 0, whole.at[a, mine, :])
        arrive("field", 1 - a, 2, whole.at[a, theirs, :])
        field_relay(a).start()

    def from_core(a):
        if a == 1:
            arrive("field", 0, 1, whole.at[1, rows_of(place_of[1]), :])
            arrive(("field relay", 1), 0, 1, whole.at[1, rows_of(place_of[3]), :])
        else:
            arrive(("field relay", a), 0, 1, whole.at[a, other_pair, :])

    y = lax.rem(lax.broadcasted_iota(jnp.int32, (1, NXY), 1), NY)

    def keep(values, e):
        if e == 0:
            return jnp.where(y == NY - 1, 0.0, values)
        if e == 2:
            return jnp.where(y == 0, 0.0, values)
        return values

    def shifted(b, e):
        start = PAD + NY * (b - 1) + (e - 1)
        return slice(start, start + NXY)

    def wide(column):
        return jnp.concatenate([column] * (NXY // 128), axis=1)

    def convolve(k, place):
        rows = pl.ds(pl.multiple_of(place * units, units), units)
        one = lax.dot_general(
            wf[k, place], patches[...], (((0,), (0,)), ((), ())), preferred_element_type=F32
        )
        hidden[rows, :] = jnp.maximum(one, 0.0).astype(BF16)

    for k in range(STEPS):
        if k == 0:
            for a in (1, 0, 2):
                on_side(a, lambda a=a: from_columns(a))
        for a in (1, 0, 2):
            if k == 0:
                on_side(a, lambda a=a: from_core(a))
                plane = whole[a]
            else:
                for j in (1, 2, 3, 0):
                    if a == 1 and j == 0:
                        continue
                    on_side(
                        a, lambda a=a, j=j: arrive("coupled", 1 - a, j, cgot.at[a, place_of[j]])
                    )
                got = [cgot[a, s].astype(F32) for s in range(n_chan)]
                got = [jnp.concatenate([g[:share], g[share:]], axis=1) for g in got]
                plane = jnp.concatenate([fronts[a]] + got, axis=0).astype(BF16)
            if a == 1:
                permuted = jnp.dot(perm[k], plane, preferred_element_type=F32)
                back[...] = permuted
                front = permuted[:HALF]
            else:
                front = jnp.dot(perm[k, 0:HALF, :], plane, preferred_element_type=F32)
            if k == 0:
                fronts[a] = front
            for e in range(3):
                xpad[e, a * HALF : (a + 1) * HALF, PAD : PAD + NXY] = keep(front, e).astype(BF16)
            for b in range(3):
                for e in range(3):
                    at = ((a * 3 + b) * 3 + e) * HALF
                    patches[at : at + HALF, :] = xpad[e, a * HALF : (a + 1) * HALF, shifted(b, e)]
        if k == 0:
            convolve(0, c)
            loads[2].wait()
            first_arrives(0, 0)
            first_relay(0, 0).start()
            for i in range(CHUNKS):
                first_copy(1, i, 2).start()
            for i in range(CHUNKS):
                arrive(("first", 0, i), 0, 1, wf.at[0, place_of[1], cuts[i], :])
            convolve(0, place_of[1])
            for i in range(1, CHUNKS):
                first_arrives(0, i)
                first_relay(0, i).start()
            convolve(0, place_of[2])
            for i in range(CHUNKS):
                part = wf.at[0, place_of[3], cuts[i], :]
                arrive(("first relay", 0, i), 0, 1, part)
            convolve(0, place_of[3])
            for load in loads[3:]:
                load.wait()
        else:
            for i in range(CHUNKS):
                arrive(("first", 1, i), 0, 1, wf.at[1, place_of[1], cuts[i], :])
                part = wf.at[1, place_of[3], cuts[i], :]
                arrive(("first relay", 1, i), 0, 1, part)
            for s in range(n_chan):
                convolve(1, s)
        summed = jnp.dot(wm[k], hidden[...], preferred_element_type=F32)
        two = jnp.maximum(summed + wide(bias2[k]), 0.0)
        for e in range(3):
            hpad[e, :, PAD : PAD + NXY] = keep(two, e).astype(BF16)
        for b in range(3):
            for e in range(3):
                at = (b * 3 + e) * units
                patches3[at : at + units, :] = hpad[e, :, shifted(b, e)]
        weights = jnp.concatenate([wl[k, i] for i in range(9)], axis=1)
        parts = jnp.dot(weights, patches3[...], preferred_element_type=F32)
        for s in range(n_chan):
            for a in range(3):
                low = a * C + s * share
                psend[k, s, a] = jnp.concatenate(
                    [parts[low : low + share], parts[low + HALF : low + HALF + share]], axis=0
                ).astype(BF16)

        def parts_copy(k, dz, j):
            return copy(
                ("parts", k), dz, j, psend.at[k, place_of[j], 1 - dz], precv.at[k, 1 - dz, c]
            )

        for dz in (-1, 1):
            when_side(
                dz, lambda dz=dz: [parts_copy(k, dz, j).start() for j in (2, 3, 1, 0)] and None
            )
        for j in (2, 3, 1):
            parts_copy(k, 0, j).start()

        precv[k, 1, c] = psend[k, c, 1]
        if k == 0:
            for i in range(CHUNKS):
                first_arrives(1, i)
                first_relay(1, i).start()
            for i in range(CHUNKS):
                first_copy(1, i, 1).start()

        for j in (1, 2, 3):
            arrive(("parts", k), 0, j, precv.at[k, 1, place_of[j]])
        net = precv[k, 1, 0].astype(F32)
        for s in range(1, n_chan):
            net = net + precv[k, 1, s].astype(F32)
        for a in (0, 2):
            for j in range(n_chan):
                on_side(
                    a,
                    lambda a=a, j=j: arrive(
                        ("parts", k), 1 - a, j, precv.at[k, a, place_of[j]]
                    ),
                )
        for a in (0, 2):
            for s in range(n_chan):
                net = net + precv[k, a, s].astype(F32)
        scales = pl.ds(pl.multiple_of(c * share, share), share)
        shifts = pl.ds(pl.multiple_of(HALF + c * share, share), share)
        arg = net[:share] + wide(bias3[k, scales, :]) + 2.0
        coupled = (back[shifts, :] + net[share:] + wide(bias3[k, shifts, :])) * jax.nn.sigmoid(arg)

        def coupled_copy(dz, j):
            return copy("coupled", dz, j, csend, cgot.at[1 - dz, c])

        if k == 0:
            packed = jnp.concatenate([coupled[:, : NXY // 2], coupled[:, NXY // 2 :]], axis=0)
            csend[...] = packed.astype(BF16)
            for dz in (-1, 1):
                when_side(
                    dz, lambda dz=dz: [coupled_copy(dz, j).start() for j in (2, 3, 1, 0)] and None
                )
            for j in (2, 3, 1):
                coupled_copy(0, j).start()
            cgot[1, c] = packed.astype(BF16)
        else:
            final_send[...] = coupled
            keeper = n_chan // 2 + lax.div(c, 2)
            place = pl.ds(pl.multiple_of(lax.rem(c, 2) * share, share), share)
            last = pltpu.make_async_remote_copy(
                src_ref=final_send,
                dst_ref=final.at[place, :],
                send_sem=send_sem.at[slot("final", 0)],
                recv_sem=recv_sem.at[slot("final", 0) + lax.rem(c, 2)],
                device_id={"chan": keeper},
                device_id_type=MESH,
            )
            slot("final", 1)

            @pl.when(keeper != c)
            def _():
                last.start()

            @pl.when(keeper == c)
            def _():
                final[place, :] = coupled

        soft = jnp.minimum(arg, 0.0) - jnp.log1p(jnp.exp(-jnp.abs(arg)))
        means = jnp.broadcast_to(jnp.sum(soft, axis=1, keepdims=True) * (1.0 / NXY), (share, share))
        diagonal = lax.broadcasted_iota(jnp.int32, (share, share), 0) == lax.broadcasted_iota(
            jnp.int32, (share, share), 1
        )
        logscale[k] = jnp.sum(jnp.where(diagonal, means, 0.0), axis=0, keepdims=True)

    for i in range(2):
        sender = 2 * (c - n_chan // 2) + i
        place = slice(i * share, (i + 1) * share)

        @pl.when(jnp.logical_and(c >= n_chan // 2, sender != c))
        def _():
            pltpu.make_async_remote_copy(
                src_ref=final_send,
                dst_ref=final.at[place, :],
                send_sem=send_sem.at[slot("final", 0)],
                recv_sem=recv_sem.at[slot("final", i)],
                device_id=peer(0, 1),
                device_id_type=MESH,
            ).wait_recv()

    @pl.when(c < n_chan // 2)
    def _():
        at = pl.ds(pl.multiple_of(lax.rem(c, 2) * own, own), own)
        final[...] = back[at, :]

    out = pltpu.make_async_copy(final, flowed.at[:, 0, :], out_sem)
    out.start()

    for dz, j in field_to:
        when_side(dz, lambda dz=dz, j=j: field_copy(dz, j).wait_send())
    for a in (0, 1, 2):
        on_side(a, lambda a=a: field_relay(a).wait_send())
    for k in range(STEPS):
        for i in range(CHUNKS):
            first_copy(k, i, 2).wait_send()
            first_copy(k, i, 1).wait_send()
            first_relay(k, i).wait_send()
        each_peer(lambda dz, j: parts_copy(k, dz, j).wait_send())
    each_peer(lambda dz, j: coupled_copy(dz, j).wait_send())

    @pl.when(n_chan // 2 + lax.div(c, 2) != c)
    def _():
        last.wait_send()

    out.wait()


def local(field, order, w_first, b_first, w_middle, b_middle, w_last, b_last):
    n_chan = lax.axis_size("chan")
    share = HALF // n_chan
    own = C // n_chan
    units = w_first.shape[1]
    vmem = pl.BlockSpec(memory_space=pltpu.VMEM)
    hbm = pl.BlockSpec(memory_space=pl.ANY)
    flowed, logscale = pl.pallas_call(
        kernel,
        out_shape=(
            jax.ShapeDtypeStruct(field.shape, F32),
            jax.ShapeDtypeStruct((STEPS, 1, share), F32),
        ),
        in_specs=[hbm, vmem, hbm, vmem, hbm, vmem, hbm, vmem],
        out_specs=(hbm, vmem),
        scratch_shapes=[
            pltpu.VMEM((own, NXY), F32),
            pltpu.VMEM((STEPS, n_chan, 27 * HALF + 16, units), BF16),
            pltpu.VMEM(w_middle.shape, BF16),
            pltpu.VMEM((STEPS, 9, 3 * C, units), BF16),
            pltpu.VMEM((STEPS, units, 128), F32),
            pltpu.VMEM((STEPS, C, 128), F32),
            pltpu.VMEM((STEPS, C, C), BF16),
            pltpu.VMEM((3, C, NXY), BF16),
            pltpu.VMEM((3, 3 * HALF, NXY + 2 * PAD), BF16),
            pltpu.VMEM((27 * HALF + 16, NXY), BF16),
            pltpu.VMEM((n_chan * units, NXY), BF16),
            pltpu.VMEM((3, units, NXY + 2 * PAD), BF16),
            pltpu.VMEM((9 * units, NXY), BF16),
            pltpu.VMEM((STEPS, n_chan, 3, 2 * share, NXY), BF16),
            pltpu.VMEM((STEPS, 3, n_chan, 2 * share, NXY), BF16),
            pltpu.VMEM((C, NXY), F32),
            pltpu.VMEM((2 * share, NXY // 2), BF16),
            pltpu.VMEM((3, n_chan, 2 * share, NXY // 2), BF16),
            pltpu.VMEM((3, HALF, NXY), F32),
            pltpu.VMEM((share, NXY), F32),
            pltpu.VMEM((own, NXY), F32),
            pltpu.SemaphoreType.DMA((10,)),
            pltpu.SemaphoreType.DMA((SEMS,)),
            pltpu.SemaphoreType.DMA((SEMS,)),
            pltpu.SemaphoreType.DMA,
        ],
        compiler_params=pltpu.CompilerParams(
            collective_id=0, has_side_effects=True, vmem_limit_bytes=62 << 20
        ),
    )(
        field, order, jnp.swapaxes(w_first, 1, 2), b_first, w_middle, b_middle,
        w_last.reshape(STEPS, 3, 9, C, units), b_last,
    )
    return flowed, jnp.swapaxes(logscale, 1, 2)


def solution(mesh):
    return jax.shard_map(
        local,
        mesh=mesh,
        in_specs=(
            P("chan", ("groups", "slab"), None),
            P(),
            P(None, "chan", None),
            P(None, "chan"),
            P(None, "chan", None),
            P(None, "chan"),
            P(None, None, "chan"),
            P(),
        ),
        out_specs=(P("chan", ("groups", "slab"), None), P(None, "chan", ("groups", "slab"))),
        check_vma=False,
    )
```

```python
import jax
import jax.numpy as jnp
from jax import lax
from jax.experimental import pallas as pl
from jax.experimental.pallas import tpu as pltpu
from jax.sharding import PartitionSpec as P
C = 64
HALF = 32
STEPS = 2
NY = 64
NXY = 512
PAD = 128
TAPS = 9 * HALF
EXTRA = 32
SPAN = TAPS + EXTRA
SEMS = 96
MESH = pl.DeviceIdType.MESH
F32 = jnp.float32
BF16 = jnp.bfloat16


def kernel(field, order, w_first, b_first, w_middle, b_middle, w_last, b_last, flowed, logscale, field_in, order_in, b1_in, b2_in, b3_in, wf, wm, wl, wl_next, bias2, bias3, perm, whole, xpad, patches, hidden, hpad, patches3, psend, precv, back, csend, cgot, fronts, net_send, net_recv, scale_send, scale_recv, net, load_sem, send_sem, recv_sem):
    n_chan = lax.axis_size('chan')
    assert n_chan == 4
    n_slab = lax.axis_size('slab')
    c = lax.axis_index('chan')
    z = lax.axis_index('slab')
    share = HALF // n_chan
    own = C // n_chan
    units = wf.shape[3]
    place_of = (c, c + 1 - 2 * lax.rem(c, 2), lax.rem(c + 2, 4), 3 - c)
    slots = {}
    started = []

    def slot(*key):
        index = slots.setdefault(key, len(slots))
        assert index < SEMS
        return index

    def peer(dz, j):
        return {'slab': z + dz, 'chan': place_of[j]}

    def inside(dz):
        return z >= -dz if dz < 0 else z < n_slab - dz

    def when_side(dz, fn):
        if dz == 0:
            fn()
        else:
            pl.when(inside(dz))(fn)

    def copy(tag, dz, j, src, dst):
        i = slot(tag, dz, j)
        return pltpu.make_async_remote_copy(src_ref=src, dst_ref=dst, send_sem=send_sem.at[i], recv_sem=recv_sem.at[i], device_id=peer(dz, j), device_id_type=MESH)

    def send(tag, dz, js, src, dst):
        copies = [copy(tag, dz, j, src(j), dst) for j in js]

        def go():
            for one in copies:
                one.start()
        when_side(dz, go)
        started.extend(((dz, one) for one in copies))

    def arrive(tag, dz, j, dst):
        i = slot(tag, dz, j)

        def wait():
            pltpu.make_async_remote_copy(src_ref=dst, dst_ref=dst, send_sem=send_sem.at[i], recv_sem=recv_sem.at[i], device_id=peer(0, 1), device_id_type=MESH).wait_recv()
        when_side(-dz, wait)
    barrier = pltpu.get_barrier_semaphore()

    def greet(device):
        pl.semaphore_signal(barrier, inc=1, device_id=device, device_id_type=MESH)
    for dz in (-1, 1):
        when_side(dz, lambda dz=dz: greet(peer(dz, 0)))
    for j in (3, 2, 1):
        greet(peer(0, j))
    loads = []

    def load(src, dst):
        one = pltpu.make_async_copy(src, dst, load_sem.at[len(loads)])
        one.start()
        loads.append(one)
        return one
    load_field = load(field.at[:, 0, :], field_in)
    load_first = [load(w_first.at[0, a], wf.at[0, c, pl.ds(a * SPAN, TAPS), :]) for a in range(3)]
    load_small = [load(order, order_in), load(b_first, b1_in), load(b_middle, b2_in), load(b_last, b3_in)]
    for e in range(3):
        xpad[e, :, 0:PAD] = jnp.zeros((5 * HALF, PAD), BF16)
        xpad[e, :, PAD + NXY:] = jnp.zeros((5 * HALF, PAD), BF16)
        hpad[e, :, 0:PAD] = jnp.zeros((units, PAD), BF16)
        hpad[e, :, PAD + NXY:] = jnp.zeros((units, PAD), BF16)
    for a in range(5):
        patches[a * SPAN + TAPS:(a + 1) * SPAN, :] = jnp.ones((EXTRA, NXY), BF16)
        if a == 2:
            continue

        @pl.when(jnp.logical_not(inside(a - 2)))
        def _():
            whole[a] = jnp.zeros((C, NXY), BF16)
            cgot[a] = jnp.zeros((n_chan, 2 * share, NXY // 2), BF16)
            if a in (1, 3):
                precv[a - 1] = jnp.zeros((n_chan, 2 * share, NXY), BF16)
    for one in load_small:
        one.wait()
    lone = lax.broadcasted_iota(jnp.int32, (EXTRA, units), 0) == 0
    for k in range(STEPS):
        bias = jnp.where(lone, b1_in[k:k + 1, :].astype(F32), 0.0).astype(BF16)
        for a in range(3):
            extra = slice(a * SPAN + TAPS, (a + 1) * SPAN)
            wf[k, c, extra, :] = bias if a == 1 else jnp.zeros_like(bias)
            if k == 0:
                blank = slice(extra.start + (16 if a == 1 else 0), extra.stop)
                for j in (1, 2, 3):
                    wf[0, place_of[j], blank, :] = jnp.zeros((blank.stop - blank.start, units), BF16)

    def rows_of(place):
        at = 2 * lax.rem(place, 2) + lax.div(place, 2)
        return pl.ds(pl.multiple_of(at * own, own), own)
    mine = rows_of(c)
    theirs = rows_of(place_of[2])
    pair = pl.ds(pl.multiple_of(lax.rem(c, 2) * 2 * own, 2 * own), 2 * own)
    other_pair = pl.ds(pl.multiple_of((1 - lax.rem(c, 2)) * 2 * own, 2 * own), 2 * own)
    load_field.wait()
    whole[2, mine, :] = field_in[...].astype(BF16)
    for one in load_first:
        one.wait()
    greeted = n_chan - 1
    for dz in (-1, 1):
        greeted = greeted + jnp.where(inside(dz), 1, 0)
    pl.semaphore_wait(barrier, greeted)

    def send_field(dz, js):
        send('field', dz, js, lambda j: whole.at[2, mine, :], whole.at[2 - dz, mine, :])

    def span(k, place, a):
        rows = SPAN if k == 1 else TAPS + 16 if a == 1 else TAPS
        return wf.at[k, place, pl.ds(a * SPAN, rows), :]

    def send_first(k, a, j):
        send(('first', k, a), 0, (j,), lambda j: span(k, c, a), span(k, c, a))

    def relay_first(k, a):
        arrive(('first', k, a), 0, 2, span(k, place_of[2], a))
        part = span(k, place_of[2], a)
        send(('first relay', k, a), 0, (1,), lambda j: part, part)

    def first_direct(k):
        for a in range(3):
            arrive(('first', k, a), 0, 1, span(k, place_of[1], a))

    def first_relayed(k):
        for a in range(3):
            arrive(('first relay', k, a), 0, 1, span(k, place_of[3], a))
    send_field(0, (2,))
    for a in range(3):
        send_first(0, a, 2)
    for dz in (-1, 1):
        send_field(dz, (0,))
    send_field(0, (1,))
    for a in range(3):
        send_first(0, a, 1)
    load_next = [load(w_first.at[1, a], wf.at[1, c, pl.ds(a * SPAN, TAPS), :]) for a in range(3)]
    load_rest = [load(w_middle, wm)]
    for a in range(3):
        for b in range(3):
            load_rest.append(load(w_last.at[1, a, b], wl_next.at[a, :, pl.ds(b * C, C), :]))
    for a in range(3):
        load_rest.append(load(w_last.at[0, a], wl.at[:, :, pl.ds(a * C, C), :]))

    def from_columns(a):
        part = whole.at[a, theirs if a == 2 else pair, :]
        if a == 2:
            arrive('field', 0, 2, part)
            for dz in (-1, 1):
                send('field pass', dz, (0,), lambda j: part, whole.at[2 - dz, theirs, :])
        elif a in (1, 3):
            arrive('field', 2 - a, 0, whole.at[a, mine, :])
            arrive('field pass', 2 - a, 0, whole.at[a, theirs, :])
        else:
            arrive('field pair', 2 - a, 0, part)
        tag = ('field relay', a)
        relay = copy(tag, 0, 1, part, part)
        when_side(a - 2, relay.start)
        started.append((a - 2, relay))

    def from_core(a):
        if a == 2:
            arrive('field', 0, 1, whole.at[2, rows_of(place_of[1]), :])
            part = whole.at[2, rows_of(place_of[3]), :]
        else:
            part = whole.at[a, other_pair, :]
        i = slot(('field relay', a), 0, 1)

        def wait():
            pltpu.make_async_remote_copy(src_ref=part, dst_ref=part, send_sem=send_sem.at[i], recv_sem=recv_sem.at[i], device_id=peer(0, 1), device_id_type=MESH).wait_recv()
        when_side(a - 2, wait)
    line = lax.broadcasted_iota(jnp.int32, (C, C), 0)

    def hits(k, channel):
        return (channel == order_in[k:k + 1, :]).astype(F32).T.astype(BF16)
    block = lax.div(line, own)
    perm[0] = hits(0, (2 * lax.rem(block, 2) + lax.div(block, 2)) * own + lax.rem(line, own))
    perm[1] = hits(1, line)
    sent = HALF + lax.div(line, 2 * share) * share + lax.rem(line, share)
    low = lax.rem(lax.div(line, share), 2) == 0
    perm[2] = hits(1, jnp.where(low, sent, -1))
    perm[3] = hits(1, jnp.where(low, -1, sent))
    for k in range(STEPS):
        bias2[k] = jnp.broadcast_to(b2_in[k:k + 1, :].astype(F32), (128, units)).T
        bias3[k] = jnp.broadcast_to(b3_in[k:k + 1, :].astype(F32), (128, C)).T
    y = lax.rem(lax.broadcasted_iota(jnp.int32, (1, NXY), 1), NY)
    lane = lax.broadcasted_iota(jnp.int32, (1, NXY), 1)

    def keep(values, e):
        if e == 0:
            return jnp.where(y == NY - 1, 0.0, values)
        if e == 2:
            return jnp.where(y == 0, 0.0, values)
        return values

    def shifted(b, e):
        start = PAD + NY * (b - 1) + (e - 1)
        return slice(start, start + NXY)

    def wide(column):
        return jnp.concatenate([column.astype(F32)] * (NXY // 128), axis=1)

    def lay(a, front):
        for e in range(3):
            xpad[e, a * HALF:(a + 1) * HALF, PAD:PAD + NXY] = keep(front, e).astype(BF16)
        for b in range(3):
            for e in range(3):
                at = a * SPAN + (b * 3 + e) * HALF
                patches[at:at + HALF, :] = xpad[e, a * HALF:(a + 1) * HALF, shifted(b, e)]

    def convolve(k, place, p):
        rows = place * units if isinstance(place, int) else pl.multiple_of(place * units, units)
        one = lax.dot_general(wf[k, place], patches[p * SPAN:(p + 3) * SPAN, :], (((0,), (0,)), ((), ())), preferred_element_type=F32)
        hidden[p, pl.ds(rows, units), :] = jnp.maximum(one, 0.0).astype(BF16)

    def finish():
        for dz, one in started:
            when_side(dz, one.wait_send)
    from_columns(2)
    for one in load_next:
        one.wait()
    relay_first(0, 0)
    for a in range(3):
        send_first(1, a, 2)
    for a in (1, 3):
        from_columns(a)
    relay_first(0, 1)
    for a in (2, 1, 3):
        from_core(a)
        if a == 2:
            permuted = jnp.dot(perm[0], whole[2], preferred_element_type=F32)
            back[...] = permuted
            front = permuted[:HALF]
        else:
            front = jnp.dot(perm[0, 0:HALF, :], whole[a], preferred_element_type=F32)
        fronts[a] = front.astype(BF16)
        lay(a, front)
    convolve(0, c, 1)
    first_direct(0)
    convolve(0, place_of[1], 1)
    relay_first(0, 2)
    convolve(0, place_of[2], 1)
    first_relayed(0)
    convolve(0, place_of[3], 1)
    for one in load_rest:
        one.wait()
    summed = jnp.dot(wm[0], hidden[1], preferred_element_type=F32)
    two = jnp.maximum(summed + wide(bias2[0]), 0.0)
    for e in range(3):
        hpad[e, :, PAD:PAD + NXY] = keep(two, e).astype(BF16)
    for b in range(3):
        for e in range(3):
            at = (b * 3 + e) * units
            patches3[at:at + units, :] = hpad[e, :, shifted(b, e)]
    weights = jnp.concatenate([wl[b, e] for b in range(3) for e in range(3)], axis=1)
    parts = jnp.dot(weights, patches3[...], preferred_element_type=F32)
    for s in range(n_chan):
        for a in range(3):
            at = a * C + s * share
            psend[s, a] = jnp.concatenate([parts[at:at + share], parts[at + HALF:at + HALF + share]], axis=0).astype(BF16)
    for dz in (-1, 1):
        send('parts', dz, (2, 3, 1, 0), lambda j: psend.at[place_of[j], 1 - dz], precv.at[1 - dz, c])
    send('parts', 0, (2, 3, 1), lambda j: psend.at[place_of[j], 1], precv.at[1, c])
    precv[1, c] = psend[c, 1]
    for dz in (-2, 2):
        send('field pair', dz, (0,), lambda j: whole.at[2, pair, :], whole.at[2 - dz, pair, :])
    for a in range(3):
        relay_first(1, a)
    for a in range(3):
        send_first(1, a, 1)
    for a in (0, 4):
        from_columns(a)
    for j in (1, 2, 3):
        arrive('parts', 0, j, precv.at[1, place_of[j]])
    total = precv[1, 0].astype(F32)
    for s in range(1, n_chan):
        total = total + precv[1, s].astype(F32)
    for a in (0, 2):
        for j in range(n_chan):
            arrive('parts', 1 - a, j, precv.at[a, place_of[j]])
    for a in (0, 2):
        for s in range(n_chan):
            total = total + precv[a, s].astype(F32)
    scales = pl.ds(pl.multiple_of(c * share, share), share)
    shifts = pl.ds(pl.multiple_of(HALF + c * share, share), share)
    arg = total[:share] + wide(bias3[0, scales, :]) + 2.0
    coupled = (back[shifts, :] + total[share:] + wide(bias3[0, shifts, :])) * jax.nn.sigmoid(arg)
    packed = jnp.concatenate([coupled[:, :NXY // 2], coupled[:, NXY // 2:]], axis=0)
    csend[...] = packed.astype(BF16)
    for dz in (-2, 2, -1, 1):
        send('coupled', dz, (3, 2, 0, 1), lambda j: csend, cgot.at[2 - dz, c])
    send('coupled', 0, (3, 2, 1), lambda j: csend, cgot.at[2, c])
    cgot[2, c] = packed.astype(BF16)

    def log_means(k, arg):
        soft = jnp.minimum(arg, 0.0) - jnp.log1p(jnp.exp(-jnp.abs(arg)))
        means = jnp.broadcast_to(jnp.sum(soft, axis=1, keepdims=True) * (1.0 / NXY), (share, share))
        diagonal = lax.broadcasted_iota(jnp.int32, (share, share), 0) == lax.broadcasted_iota(jnp.int32, (share, share), 1)
        logscale[k] = jnp.sum(jnp.where(diagonal, means, 0.0), axis=0, keepdims=True)
    log_means(0, arg)
    for a in (0, 4):
        from_core(a)
        front = jnp.dot(perm[0, 0:HALF, :], whole[a], preferred_element_type=F32)
        fronts[a] = front.astype(BF16)
    first_direct(1)
    first_relayed(1)

    def front_of(a, rows):
        kept = jnp.dot(perm[1, 0:rows, 0:HALF], fronts[a], preferred_element_type=F32)
        got = jnp.concatenate([cgot[a, s] for s in range(n_chan)], axis=0)
        halves = [jnp.dot(perm[i, 0:rows, :], got, preferred_element_type=F32) for i in (2, 3)]
        return kept + jnp.concatenate(halves, axis=1)

    def coupled_arrives(a):
        for j in (1, 2, 3, 0):
            if (a, j) != (2, 0):
                arrive('coupled', 2 - a, j, cgot.at[a, place_of[j]])
    for a in (2, 1, 3):
        coupled_arrives(a)
        if a == 2:
            permuted = front_of(2, C)
            back[...] = permuted
            front = permuted[:HALF]
        else:
            front = front_of(a, HALF)
        lay(a, front)
    for s in range(n_chan):
        convolve(1, s, 1)
    for a in (0, 4):
        coupled_arrives(a)
        lay(a, front_of(a, HALF))
    for p in (0, 2):
        for s in range(n_chan):
            convolve(1, s, p)
    for p in (1, 0, 2):
        two = jnp.maximum(jnp.dot(wm[1], hidden[p], preferred_element_type=F32) + wide(bias2[1]), 0.0)
        if p != 1:
            two = jnp.where(inside(p - 1), two, 0.0)
        left = jnp.where(y == 0, 0.0, pltpu.roll(two, 1, 1))
        right = jnp.where(y == NY - 1, 0.0, pltpu.roll(two, NXY - 1, 1))
        for e, values in enumerate((left, two, right)):
            at = (3 * p + e) * units
            patches3[at:at + units, :] = values.astype(BF16)
    weights = jnp.concatenate([wl_next[a, e] for a in range(3) for e in range(3)], axis=1)
    parts = jnp.dot(weights, patches3[...], preferred_element_type=F32)
    part = parts[C:2 * C]
    part = part + jnp.where(lane < NY, 0.0, pltpu.roll(parts[0:C], NY, 1))
    part = part + jnp.where(lane >= NXY - NY, 0.0, pltpu.roll(parts[2 * C:], NXY - NY, 1))
    for i in range(2):
        at = i * own
        net_send[i] = jnp.concatenate([part[at:at + own], part[HALF + at:HALF + at + own]], axis=0).astype(BF16)
    for s in range(n_chan):
        rows = part[s * share:(s + 1) * share]
        scale_send[s] = jnp.concatenate([rows[:, :NXY // 2], rows[:, NXY // 2:]], axis=0).astype(BF16)
    nets = []
    for j in (3, 2, 1):
        to = place_of[j]
        one = copy('net', 0, j, net_send.at[lax.rem(to, 2)], net_recv.at[j])
        nets.append((to, one))
        pl.when(to >= n_chan // 2)(one.start)
        send('scale', 0, (j,), lambda j: scale_send.at[place_of[j]], scale_recv.at[j])
    net[...] = part + wide(bias3[1])
    kept = pl.ds(pl.multiple_of(lax.rem(c, 2) * own, own), own)
    moved = pl.ds(pl.multiple_of(HALF + lax.rem(c, 2) * own, own), own)

    @pl.when(c < n_chan // 2)
    def _():
        flowed[...] = back[kept, :]

    @pl.when(c >= n_chan // 2)
    def _():
        scaled, added = (net[kept, :], net[moved, :])
        for j in (1, 2, 3):
            arrive('net', 0, j, net_recv.at[j])
            got = net_recv[j].astype(F32)
            scaled, added = (scaled + got[:own], added + got[own:])
        flowed[...] = (back[moved, :] + added) * jax.nn.sigmoid(scaled + 2.0)
    arg = net[scales, :] + 2.0
    for j in (1, 2, 3):
        arrive('scale', 0, j, scale_recv.at[j])
        got = scale_recv[j].astype(F32)
        arg = arg + jnp.concatenate([got[:share], got[share:]], axis=1)
    log_means(1, arg)
    for to, one in nets:
        pl.when(to >= n_chan // 2)(one.wait_send)
    finish()


def store(moved, means, flowed, logscale):
    flowed[:, 0, :] = moved[...]
    logscale[...] = means[...]


def local(field, order, w_first, b_first, w_middle, b_middle, w_last, b_last):
    n_chan = lax.axis_size('chan')
    share = HALF // n_chan
    own = C // n_chan
    units = w_first.shape[1]
    vmem = pl.BlockSpec(memory_space=pltpu.VMEM)
    hbm = pl.BlockSpec(memory_space=pl.ANY)
    moved, means = pl.pallas_call(kernel, out_shape=(pltpu.VMEM((own, NXY), F32), pltpu.VMEM((STEPS, 1, share), F32)), in_specs=[hbm] * 8, out_specs=(vmem, vmem), scratch_shapes=[pltpu.VMEM((own, NXY), F32), pltpu.VMEM(order.shape, jnp.int32), pltpu.VMEM(b_first.shape, BF16), pltpu.VMEM(b_middle.shape, BF16), pltpu.VMEM(b_last.shape, BF16), pltpu.VMEM((STEPS, n_chan, 3 * SPAN, units), BF16), pltpu.VMEM((STEPS, units, n_chan * units), BF16), pltpu.VMEM((3, 3, 3 * C, units), BF16), pltpu.VMEM((3, 3, 3 * C, units), BF16), pltpu.VMEM((STEPS, units, 128), F32), pltpu.VMEM((STEPS, C, 128), F32), pltpu.VMEM((4, C, C), BF16), pltpu.VMEM((5, C, NXY), BF16), pltpu.VMEM((3, 5 * HALF, NXY + 2 * PAD), BF16), pltpu.VMEM((5 * SPAN, NXY), BF16), pltpu.VMEM((3, n_chan * units, NXY), BF16), pltpu.VMEM((3, units, NXY + 2 * PAD), BF16), pltpu.VMEM((9 * units, NXY), BF16), pltpu.VMEM((n_chan, 3, 2 * share, NXY), BF16), pltpu.VMEM((3, n_chan, 2 * share, NXY), BF16), pltpu.VMEM((C, NXY), F32), pltpu.VMEM((2 * share, NXY // 2), BF16), pltpu.VMEM((5, n_chan, 2 * share, NXY // 2), BF16), pltpu.VMEM((5, HALF, NXY), BF16), pltpu.VMEM((2, 2 * own, NXY), BF16), pltpu.VMEM((n_chan, 2 * own, NXY), BF16), pltpu.VMEM((n_chan, 2 * share, NXY // 2), BF16), pltpu.VMEM((n_chan, 2 * share, NXY // 2), BF16), pltpu.VMEM((C, NXY), F32), pltpu.SemaphoreType.DMA((32,)), pltpu.SemaphoreType.DMA((SEMS,)), pltpu.SemaphoreType.DMA((SEMS,))], compiler_params=pltpu.CompilerParams(collective_id=0, has_side_effects=True, vmem_limit_bytes=62 << 20))(field, order, jnp.swapaxes(w_first, 1, 2).reshape(STEPS, 3, TAPS, units), b_first, w_middle, b_middle, w_last.reshape(STEPS, 3, 3, 3, C, units), b_last)
    moved, means = (pltpu.with_memory_space_constraint(v, pltpu.VMEM) for v in (moved, means))
    flowed, logscale = pl.pallas_call(store, out_shape=(jax.ShapeDtypeStruct(field.shape, F32), jax.ShapeDtypeStruct((STEPS, 1, share), F32)), in_specs=[vmem, vmem], out_specs=(vmem, vmem))(moved, means)
    return (flowed, jnp.swapaxes(logscale, 1, 2))


def solution(mesh):
    return jax.shard_map(local, mesh=mesh, in_specs=(P('chan', ('groups', 'slab'), None), P(), P(None, 'chan', None), P(None, 'chan'), P(None, 'chan', None), P(None, 'chan'), P(None, None, 'chan'), P()), out_specs=(P('chan', ('groups', 'slab'), None), P(None, 'chan', ('groups', 'slab'))), check_vma=False)
```

```python
import jax
import jax.numpy as jnp
from jax import lax
from jax.experimental import pallas as pl
from jax.experimental.pallas import tpu as pltpu
from jax.sharding import PartitionSpec as P
C = 64
HALF = 32
STEPS = 2
NY = 64
NXY = 512
PAD = 128
TAPS = 9 * HALF
EXTRA = 32
SPAN = TAPS + EXTRA
SEMS = 96
MESH = pl.DeviceIdType.MESH
F32 = jnp.float32
BF16 = jnp.bfloat16


def kernel(field, order, w_first, b_first, w_middle, b_middle, w_last, b_last, flowed, logscale, field_in, order_in, b1_in, b2_in, b3_in, wf, wm, wl, wl_next, bias2, bias3, perm, whole, xpad, patches, hidden, hpad, patches3, psend, precv, back, csend, cgot, fronts, net_send, net_recv, scale_send, scale_recv, net, load_sem, send_sem, recv_sem):
    n_chan = lax.axis_size('chan')
    assert n_chan == 4
    n_slab = lax.axis_size('slab')
    c = lax.axis_index('chan')
    z = lax.axis_index('slab')
    share = HALF // n_chan
    own = C // n_chan
    units = wf.shape[3]
    place_of = (c, c + 1 - 2 * lax.rem(c, 2), lax.rem(c + 2, 4), 3 - c)
    slots = {}
    started = []

    def slot(*key):
        index = slots.setdefault(key, len(slots))
        assert index < SEMS
        return index

    def peer(dz, j):
        return {'slab': z + dz, 'chan': place_of[j]}

    def inside(dz):
        return z >= -dz if dz < 0 else z < n_slab - dz

    def when_side(dz, fn):
        if dz == 0:
            fn()
        else:
            pl.when(inside(dz))(fn)

    def copy(tag, dz, j, src, dst):
        i = slot(tag, dz, j)
        return pltpu.make_async_remote_copy(src_ref=src, dst_ref=dst, send_sem=send_sem.at[i], recv_sem=recv_sem.at[i], device_id=peer(dz, j), device_id_type=MESH)

    def send(tag, dz, js, src, dst):
        copies = [copy(tag, dz, j, src(j), dst) for j in js]

        def go():
            for one in copies:
                one.start()
        when_side(dz, go)
        started.extend(((dz, one) for one in copies))

    def arrive(tag, dz, j, dst):
        i = slot(tag, dz, j)

        def wait():
            pltpu.make_async_remote_copy(src_ref=dst, dst_ref=dst, send_sem=send_sem.at[i], recv_sem=recv_sem.at[i], device_id=peer(0, 1), device_id_type=MESH).wait_recv()
        when_side(-dz, wait)
    barrier = pltpu.get_barrier_semaphore()

    def greet(device):
        pl.semaphore_signal(barrier, inc=1, device_id=device, device_id_type=MESH)
    for dz in (-1, 1):
        when_side(dz, lambda dz=dz: greet(peer(dz, 0)))
    for j in (3, 2, 1):
        greet(peer(0, j))
    loads = []

    def load(src, dst):
        one = pltpu.make_async_copy(src, dst, load_sem.at[len(loads)])
        one.start()
        loads.append(one)
        return one
    load_field = load(field.at[:, 0, :], field_in)
    load_first = [load(w_first.at[0, a], wf.at[0, c, pl.ds(a * SPAN, TAPS), :]) for a in range(3)]
    load_small = [load(order, order_in), load(b_first, b1_in), load(b_middle, b2_in), load(b_last, b3_in)]
    for e in range(3):
        xpad[e, :, 0:PAD] = jnp.zeros((5 * HALF, PAD), BF16)
        xpad[e, :, PAD + NXY:] = jnp.zeros((5 * HALF, PAD), BF16)
        hpad[e, :, 0:PAD] = jnp.zeros((units, PAD), BF16)
        hpad[e, :, PAD + NXY:] = jnp.zeros((units, PAD), BF16)
    for a in range(5):
        patches[a * SPAN + TAPS:(a + 1) * SPAN, :] = jnp.ones((EXTRA, NXY), BF16)
        if a == 2:
            continue

        @pl.when(jnp.logical_not(inside(a - 2)))
        def _():
            whole[a] = jnp.zeros((C, NXY), BF16)
            cgot[a] = jnp.zeros((n_chan, 2 * share, NXY // 2), BF16)
            if a in (1, 3):
                precv[a - 1] = jnp.zeros((n_chan, 2 * share, NXY), BF16)
    for one in load_small:
        one.wait()
    lone = lax.broadcasted_iota(jnp.int32, (EXTRA, units), 0) == 0
    for k in range(STEPS):
        bias = jnp.where(lone, b1_in[k:k + 1, :].astype(F32), 0.0).astype(BF16)
        for a in range(3):
            extra = slice(a * SPAN + TAPS, (a + 1) * SPAN)
            wf[k, c, extra, :] = bias if a == 1 else jnp.zeros_like(bias)
            if k == 0:
                blank = slice(extra.start + (16 if a == 1 else 0), extra.stop)
                for j in (1, 2, 3):
                    wf[0, place_of[j], blank, :] = jnp.zeros((blank.stop - blank.start, units), BF16)

    def rows_of(place):
        at = 2 * lax.rem(place, 2) + lax.div(place, 2)
        return pl.ds(pl.multiple_of(at * own, own), own)
    mine = rows_of(c)
    theirs = rows_of(place_of[2])
    pair = pl.ds(pl.multiple_of(lax.rem(c, 2) * 2 * own, 2 * own), 2 * own)
    other_pair = pl.ds(pl.multiple_of((1 - lax.rem(c, 2)) * 2 * own, 2 * own), 2 * own)
    load_field.wait()
    whole[2, mine, :] = field_in[...].astype(BF16)
    for one in load_first:
        one.wait()
    greeted = n_chan - 1
    for dz in (-1, 1):
        greeted = greeted + jnp.where(inside(dz), 1, 0)
    pl.semaphore_wait(barrier, greeted)

    def send_field(dz, js):
        send('field', dz, js, lambda j: whole.at[2, mine, :], whole.at[2 - dz, mine, :])

    def span(k, place, a):
        rows = SPAN if k == 1 else TAPS + 16 if a == 1 else TAPS
        return wf.at[k, place, pl.ds(a * SPAN, rows), :]

    def send_first(k, a, j):
        send(('first', k, a), 0, (j,), lambda j: span(k, c, a), span(k, c, a))

    def relay_first(k, a):
        arrive(('first', k, a), 0, 2, span(k, place_of[2], a))
        part = span(k, place_of[2], a)
        send(('first relay', k, a), 0, (1,), lambda j: part, part)

    def first_direct(k):
        for a in range(3):
            arrive(('first', k, a), 0, 1, span(k, place_of[1], a))

    def first_relayed(k):
        for a in range(3):
            arrive(('first relay', k, a), 0, 1, span(k, place_of[3], a))
    send_field(0, (2,))
    for a in range(3):
        send_first(0, a, 2)
    for dz in (-1, 1):
        send_field(dz, (0,))
    send_field(0, (1,))
    for a in range(3):
        send_first(0, a, 1)
    load_next = [load(w_first.at[1, a], wf.at[1, c, pl.ds(a * SPAN, TAPS), :]) for a in range(3)]
    load_rest = [load(w_middle, wm)]
    for a in range(3):
        for b in range(3):
            load_rest.append(load(w_last.at[1, a, b], wl_next.at[a, :, pl.ds(b * C, C), :]))
    for a in range(3):
        load_rest.append(load(w_last.at[0, a], wl.at[:, :, pl.ds(a * C, C), :]))

    def from_columns(a):
        part = whole.at[a, theirs if a == 2 else pair, :]
        if a == 2:
            arrive('field', 0, 2, part)
            for dz in (-1, 1):
                send('field pass', dz, (0,), lambda j: part, whole.at[2 - dz, theirs, :])
        elif a in (1, 3):
            arrive('field', 2 - a, 0, whole.at[a, mine, :])
            arrive('field pass', 2 - a, 0, whole.at[a, theirs, :])
        else:
            arrive('field pair', 2 - a, 0, part)
        tag = ('field relay', a)
        relay = copy(tag, 0, 1, part, part)
        when_side(a - 2, relay.start)
        started.append((a - 2, relay))

    def from_core(a):
        if a == 2:
            arrive('field', 0, 1, whole.at[2, rows_of(place_of[1]), :])
            part = whole.at[2, rows_of(place_of[3]), :]
        else:
            part = whole.at[a, other_pair, :]
        i = slot(('field relay', a), 0, 1)

        def wait():
            pltpu.make_async_remote_copy(src_ref=part, dst_ref=part, send_sem=send_sem.at[i], recv_sem=recv_sem.at[i], device_id=peer(0, 1), device_id_type=MESH).wait_recv()
        when_side(a - 2, wait)
    line = lax.broadcasted_iota(jnp.int32, (C, C), 0)

    def hits(k, channel):
        return (channel == order_in[k:k + 1, :]).astype(F32).T.astype(BF16)
    block = lax.div(line, own)
    perm[0] = hits(0, (2 * lax.rem(block, 2) + lax.div(block, 2)) * own + lax.rem(line, own))
    perm[1] = hits(1, line)
    sent = HALF + lax.div(line, 2 * share) * share + lax.rem(line, share)
    low = lax.rem(lax.div(line, share), 2) == 0
    perm[2] = hits(1, jnp.where(low, sent, -1))
    perm[3] = hits(1, jnp.where(low, -1, sent))
    for k in range(STEPS):
        bias2[k] = jnp.broadcast_to(b2_in[k:k + 1, :].astype(F32), (128, units)).T
        bias3[k] = jnp.broadcast_to(b3_in[k:k + 1, :].astype(F32), (128, C)).T
    y = lax.rem(lax.broadcasted_iota(jnp.int32, (1, NXY), 1), NY)
    lane = lax.broadcasted_iota(jnp.int32, (1, NXY), 1)

    def keep(values, e):
        if e == 0:
            return jnp.where(y == NY - 1, 0.0, values)
        if e == 2:
            return jnp.where(y == 0, 0.0, values)
        return values

    def shifted(b, e):
        start = PAD + NY * (b - 1) + (e - 1)
        return slice(start, start + NXY)

    def wide(column):
        return jnp.concatenate([column.astype(F32)] * (NXY // 128), axis=1)

    def lay(a, front):
        for e in range(3):
            xpad[e, a * HALF:(a + 1) * HALF, PAD:PAD + NXY] = keep(front, e).astype(BF16)
        for b in range(3):
            for e in range(3):
                at = a * SPAN + (b * 3 + e) * HALF
                patches[at:at + HALF, :] = xpad[e, a * HALF:(a + 1) * HALF, shifted(b, e)]

    def convolve(k, place, p):
        rows = place * units if isinstance(place, int) else pl.multiple_of(place * units, units)
        one = lax.dot_general(wf[k, place], patches[p * SPAN:(p + 3) * SPAN, :], (((0,), (0,)), ((), ())), preferred_element_type=F32)
        hidden[p, pl.ds(rows, units), :] = jnp.maximum(one, 0.0).astype(BF16)

    def finish():
        for dz, one in started:
            when_side(dz, one.wait_send)
    from_columns(2)
    for one in load_next:
        one.wait()
    relay_first(0, 0)
    for a in range(3):
        send_first(1, a, 2)
    for a in (1, 3):
        from_columns(a)
    relay_first(0, 1)
    for dz in (-2, 2):
        send('field pair', dz, (0,), lambda j: whole.at[2, pair, :], whole.at[2 - dz, pair, :])
    relay_first(0, 2)
    for a in (2, 1, 3):
        from_core(a)
        if a == 2:
            permuted = jnp.dot(perm[0], whole[2], preferred_element_type=F32)
            back[...] = permuted
            front = permuted[:HALF]
        else:
            front = jnp.dot(perm[0, 0:HALF, :], whole[a], preferred_element_type=F32)
        fronts[a] = front.astype(BF16)
        lay(a, front)
    convolve(0, c, 1)
    first_direct(0)
    convolve(0, place_of[1], 1)
    convolve(0, place_of[2], 1)
    first_relayed(0)
    convolve(0, place_of[3], 1)
    for one in load_rest:
        one.wait()
    summed = jnp.dot(wm[0], hidden[1], preferred_element_type=F32)
    two = jnp.maximum(summed + wide(bias2[0]), 0.0)
    for e in range(3):
        hpad[e, :, PAD:PAD + NXY] = keep(two, e).astype(BF16)
    for b in range(3):
        for e in range(3):
            at = (b * 3 + e) * units
            patches3[at:at + units, :] = hpad[e, :, shifted(b, e)]
    weights = jnp.concatenate([wl[b, e] for b in range(3) for e in range(3)], axis=1)
    parts = jnp.dot(weights, patches3[...], preferred_element_type=F32)
    for s in range(n_chan):
        for a in range(3):
            at = a * C + s * share
            psend[s, a] = jnp.concatenate([parts[at:at + share], parts[at + HALF:at + HALF + share]], axis=0).astype(BF16)
    for dz in (-1, 1):
        send('parts', dz, (2, 3, 1, 0), lambda j: psend.at[place_of[j], 1 - dz], precv.at[1 - dz, c])
    send('parts', 0, (2, 3, 1), lambda j: psend.at[place_of[j], 1], precv.at[1, c])
    precv[1, c] = psend[c, 1]
    for a in range(3):
        relay_first(1, a)
    for a in range(3):
        send_first(1, a, 1)
    for a in (0, 4):
        from_columns(a)
    for j in (1, 2, 3):
        arrive('parts', 0, j, precv.at[1, place_of[j]])
    total = precv[1, 0].astype(F32)
    for s in range(1, n_chan):
        total = total + precv[1, s].astype(F32)
    for a in (0, 2):
        for j in range(n_chan):
            arrive('parts', 1 - a, j, precv.at[a, place_of[j]])
    for a in (0, 2):
        for s in range(n_chan):
            total = total + precv[a, s].astype(F32)
    scales = pl.ds(pl.multiple_of(c * share, share), share)
    shifts = pl.ds(pl.multiple_of(HALF + c * share, share), share)
    arg = total[:share] + wide(bias3[0, scales, :]) + 2.0
    coupled = (back[shifts, :] + total[share:] + wide(bias3[0, shifts, :])) * jax.nn.sigmoid(arg)
    packed = jnp.concatenate([coupled[:, :NXY // 2], coupled[:, NXY // 2:]], axis=0)
    csend[...] = packed.astype(BF16)
    for dz in (-2, 2, -1, 1):
        send('coupled', dz, (3, 2, 0, 1), lambda j: csend, cgot.at[2 - dz, c])
    send('coupled', 0, (3, 2, 1), lambda j: csend, cgot.at[2, c])
    cgot[2, c] = packed.astype(BF16)

    def log_means(k, arg):
        soft = jnp.minimum(arg, 0.0) - jnp.log1p(jnp.exp(-jnp.abs(arg)))
        means = jnp.broadcast_to(jnp.sum(soft, axis=1, keepdims=True) * (1.0 / NXY), (share, share))
        diagonal = lax.broadcasted_iota(jnp.int32, (share, share), 0) == lax.broadcasted_iota(jnp.int32, (share, share), 1)
        logscale[k] = jnp.sum(jnp.where(diagonal, means, 0.0), axis=0, keepdims=True)
    log_means(0, arg)
    for a in (0, 4):
        from_core(a)
        front = jnp.dot(perm[0, 0:HALF, :], whole[a], preferred_element_type=F32)
        fronts[a] = front.astype(BF16)
    first_direct(1)
    first_relayed(1)

    def front_of(a, rows):
        kept = jnp.dot(perm[1, 0:rows, 0:HALF], fronts[a], preferred_element_type=F32)
        got = jnp.concatenate([cgot[a, s] for s in range(n_chan)], axis=0)
        halves = [jnp.dot(perm[i, 0:rows, :], got, preferred_element_type=F32) for i in (2, 3)]
        return kept + jnp.concatenate(halves, axis=1)

    def coupled_arrives(a):
        for j in (1, 2, 3, 0):
            if (a, j) != (2, 0):
                arrive('coupled', 2 - a, j, cgot.at[a, place_of[j]])
    for a in (2, 1, 3):
        coupled_arrives(a)
        if a == 2:
            permuted = front_of(2, C)
            back[...] = permuted
            front = permuted[:HALF]
        else:
            front = front_of(a, HALF)
        lay(a, front)
    for s in range(n_chan):
        convolve(1, s, 1)
    for a in (0, 4):
        coupled_arrives(a)
        lay(a, front_of(a, HALF))
    for p in (0, 2):
        for s in range(n_chan):
            convolve(1, s, p)
    for p in (1, 0, 2):
        two = jnp.maximum(jnp.dot(wm[1], hidden[p], preferred_element_type=F32) + wide(bias2[1]), 0.0)
        if p != 1:
            two = jnp.where(inside(p - 1), two, 0.0)
        left = jnp.where(y == 0, 0.0, pltpu.roll(two, 1, 1))
        right = jnp.where(y == NY - 1, 0.0, pltpu.roll(two, NXY - 1, 1))
        for e, values in enumerate((left, two, right)):
            at = (3 * p + e) * units
            patches3[at:at + units, :] = values.astype(BF16)
    weights = jnp.concatenate([wl_next[a, e] for a in range(3) for e in range(3)], axis=1)
    parts = jnp.dot(weights, patches3[...], preferred_element_type=F32)
    part = parts[C:2 * C]
    part = part + jnp.where(lane < NY, 0.0, pltpu.roll(parts[0:C], NY, 1))
    part = part + jnp.where(lane >= NXY - NY, 0.0, pltpu.roll(parts[2 * C:], NXY - NY, 1))
    for i in range(2):
        at = i * own
        net_send[i] = jnp.concatenate([part[at:at + own], part[HALF + at:HALF + at + own]], axis=0).astype(BF16)
    for s in range(n_chan):
        rows = part[s * share:(s + 1) * share]
        scale_send[s] = jnp.concatenate([rows[:, :NXY // 2], rows[:, NXY // 2:]], axis=0).astype(BF16)
    nets = []
    for j in (3, 2, 1):
        to = place_of[j]
        one = copy('net', 0, j, net_send.at[lax.rem(to, 2)], net_recv.at[j])
        nets.append((to, one))
        pl.when(to >= n_chan // 2)(one.start)
        send('scale', 0, (j,), lambda j: scale_send.at[place_of[j]], scale_recv.at[j])
    net[...] = part + wide(bias3[1])
    kept = pl.ds(pl.multiple_of(lax.rem(c, 2) * own, own), own)
    moved = pl.ds(pl.multiple_of(HALF + lax.rem(c, 2) * own, own), own)

    @pl.when(c < n_chan // 2)
    def _():
        flowed[...] = back[kept, :]

    @pl.when(c >= n_chan // 2)
    def _():
        scaled, added = (net[kept, :], net[moved, :])
        for j in (1, 2, 3):
            arrive('net', 0, j, net_recv.at[j])
            got = net_recv[j].astype(F32)
            scaled, added = (scaled + got[:own], added + got[own:])
        flowed[...] = (back[moved, :] + added) * jax.nn.sigmoid(scaled + 2.0)
    arg = net[scales, :] + 2.0
    for j in (1, 2, 3):
        arrive('scale', 0, j, scale_recv.at[j])
        got = scale_recv[j].astype(F32)
        arg = arg + jnp.concatenate([got[:share], got[share:]], axis=1)
    log_means(1, arg)
    for to, one in nets:
        pl.when(to >= n_chan // 2)(one.wait_send)
    finish()


def store(moved, means, flowed, logscale):
    flowed[:, 0, :] = moved[...]
    logscale[...] = means[...]


def local(field, order, w_first, b_first, w_middle, b_middle, w_last, b_last):
    n_chan = lax.axis_size('chan')
    share = HALF // n_chan
    own = C // n_chan
    units = w_first.shape[1]
    vmem = pl.BlockSpec(memory_space=pltpu.VMEM)
    hbm = pl.BlockSpec(memory_space=pl.ANY)
    moved, means = pl.pallas_call(kernel, out_shape=(pltpu.VMEM((own, NXY), F32), pltpu.VMEM((STEPS, 1, share), F32)), in_specs=[hbm] * 8, out_specs=(vmem, vmem), scratch_shapes=[pltpu.VMEM((own, NXY), F32), pltpu.VMEM(order.shape, jnp.int32), pltpu.VMEM(b_first.shape, BF16), pltpu.VMEM(b_middle.shape, BF16), pltpu.VMEM(b_last.shape, BF16), pltpu.VMEM((STEPS, n_chan, 3 * SPAN, units), BF16), pltpu.VMEM((STEPS, units, n_chan * units), BF16), pltpu.VMEM((3, 3, 3 * C, units), BF16), pltpu.VMEM((3, 3, 3 * C, units), BF16), pltpu.VMEM((STEPS, units, 128), F32), pltpu.VMEM((STEPS, C, 128), F32), pltpu.VMEM((4, C, C), BF16), pltpu.VMEM((5, C, NXY), BF16), pltpu.VMEM((3, 5 * HALF, NXY + 2 * PAD), BF16), pltpu.VMEM((5 * SPAN, NXY), BF16), pltpu.VMEM((3, n_chan * units, NXY), BF16), pltpu.VMEM((3, units, NXY + 2 * PAD), BF16), pltpu.VMEM((9 * units, NXY), BF16), pltpu.VMEM((n_chan, 3, 2 * share, NXY), BF16), pltpu.VMEM((3, n_chan, 2 * share, NXY), BF16), pltpu.VMEM((C, NXY), F32), pltpu.VMEM((2 * share, NXY // 2), BF16), pltpu.VMEM((5, n_chan, 2 * share, NXY // 2), BF16), pltpu.VMEM((5, HALF, NXY), BF16), pltpu.VMEM((2, 2 * own, NXY), BF16), pltpu.VMEM((n_chan, 2 * own, NXY), BF16), pltpu.VMEM((n_chan, 2 * share, NXY // 2), BF16), pltpu.VMEM((n_chan, 2 * share, NXY // 2), BF16), pltpu.VMEM((C, NXY), F32), pltpu.SemaphoreType.DMA((32,)), pltpu.SemaphoreType.DMA((SEMS,)), pltpu.SemaphoreType.DMA((SEMS,))], compiler_params=pltpu.CompilerParams(collective_id=0, has_side_effects=True, vmem_limit_bytes=62 << 20))(field, order, jnp.swapaxes(w_first, 1, 2).reshape(STEPS, 3, TAPS, units), b_first, w_middle, b_middle, w_last.reshape(STEPS, 3, 3, 3, C, units), b_last)
    moved, means = (pltpu.with_memory_space_constraint(v, pltpu.VMEM) for v in (moved, means))
    flowed, logscale = pl.pallas_call(store, out_shape=(jax.ShapeDtypeStruct(field.shape, F32), jax.ShapeDtypeStruct((STEPS, 1, share), F32)), in_specs=[vmem, vmem], out_specs=(vmem, vmem))(moved, means)
    return (flowed, jnp.swapaxes(logscale, 1, 2))


def solution(mesh):
    return jax.shard_map(local, mesh=mesh, in_specs=(P('chan', ('groups', 'slab'), None), P(), P(None, 'chan', None), P(None, 'chan'), P(None, 'chan', None), P(None, 'chan'), P(None, None, 'chan'), P()), out_specs=(P('chan', ('groups', 'slab'), None), P(None, 'chan', ('groups', 'slab'))), check_vma=False)
```

```python
import jax
import jax.numpy as jnp
from jax import lax
from jax.experimental import pallas as pl
from jax.experimental.pallas import tpu as pltpu
from jax.sharding import PartitionSpec as P
C = 64
HALF = 32
STEPS = 2
NY = 64
NXY = 512
PAD = 128
TAPS = 9 * HALF
EXTRA = 32
SPAN = TAPS + EXTRA
SEMS = 96
MESH = pl.DeviceIdType.MESH
F32 = jnp.float32
BF16 = jnp.bfloat16


def kernel(field, order, w_first, b_first, w_middle, b_middle, w_last, b_last, flowed, logscale, field_in, order_in, b1_in, b2_in, b3_in, wf, wm, wl, wl_next, bias2, bias3, perm, whole, xpad, patches, hidden, hpad, patches3, psend, precv, back, csend, cgot, fronts, net_send, net_recv, scale_send, scale_recv, net, b2_rows, load_sem, send_sem, recv_sem):
    n_chan = lax.axis_size('chan')
    assert n_chan == 4
    n_slab = lax.axis_size('slab')
    c = lax.axis_index('chan')
    z = lax.axis_index('slab')
    share = HALF // n_chan
    own = C // n_chan
    units = wf.shape[3]
    place_of = (c, c + 1 - 2 * lax.rem(c, 2), lax.rem(c + 2, 4), 3 - c)
    slots = {}
    started = []

    def slot(*key):
        index = slots.setdefault(key, len(slots))
        assert index < SEMS
        return index

    def peer(dz, j):
        return {'slab': z + dz, 'chan': place_of[j]}

    def inside(dz):
        return z >= -dz if dz < 0 else z < n_slab - dz

    def when_side(dz, fn):
        if dz == 0:
            fn()
        else:
            pl.when(inside(dz))(fn)

    def copy(tag, dz, j, src, dst):
        i = slot(tag, dz, j)
        return pltpu.make_async_remote_copy(src_ref=src, dst_ref=dst, send_sem=send_sem.at[i], recv_sem=recv_sem.at[i], device_id=peer(dz, j), device_id_type=MESH)

    def send(tag, dz, js, src, dst):
        copies = [copy(tag, dz, j, src(j), dst) for j in js]

        def go():
            for one in copies:
                one.start()
        when_side(dz, go)
        started.extend(((dz, one) for one in copies))

    def arrive(tag, dz, j, dst):
        i = slot(tag, dz, j)

        def wait():
            pltpu.make_async_remote_copy(src_ref=dst, dst_ref=dst, send_sem=send_sem.at[i], recv_sem=recv_sem.at[i], device_id=peer(0, 1), device_id_type=MESH).wait_recv()
        when_side(-dz, wait)
    barrier = pltpu.get_barrier_semaphore()

    def greet(device):
        pl.semaphore_signal(barrier, inc=1, device_id=device, device_id_type=MESH)
    for dz in (-1, 1):
        when_side(dz, lambda dz=dz: greet(peer(dz, 0)))
    for j in (3, 2, 1):
        greet(peer(0, j))
    far_started = []

    def send_far(tag, same, other, src, dst):
        for dz in (-2, 2):
            for js, mine_too in ((same, True), (other, False)):
                copies = [copy(tag, dz, j, src, dst) for j in js]
                wanted = jnp.logical_and(inside(dz), core == (0 if (dz == 2) == mine_too else 1))

                @pl.when(wanted)
                def _():
                    for one in copies:
                        one.start()
                far_started.extend(((wanted, one) for one in copies))

    def far_arrives(tag, j, dst):
        for dz in (-2, 2):
            i = slot(tag, dz, j)

            @pl.when(jnp.logical_and(inside(-dz), core == (0 if dz == 2 else 1)))
            def _():
                pltpu.make_async_remote_copy(src_ref=dst, dst_ref=dst, send_sem=send_sem.at[i], recv_sem=recv_sem.at[i], device_id=peer(0, 1), device_id_type=MESH).wait_recv()
    core = lax.rem(c, 2)
    loads = []

    def load(src, dst):
        one = pltpu.make_async_copy(src, dst, load_sem.at[len(loads)])
        one.start()
        loads.append(one)
        return one
    load_field = load(field.at[:, 0, :], field_in)
    load_first = [load(w_first.at[0, a], wf.at[0, c, pl.ds(a * SPAN, TAPS), :]) for a in range(3)]
    load_small = [load(order, order_in), load(b_first, b1_in), load(b_middle, b2_in), load(b_last, b3_in)]
    for e in range(3):
        xpad[e, :, 0:PAD] = jnp.zeros((5 * HALF, PAD), BF16)
        xpad[e, :, PAD + NXY:] = jnp.zeros((5 * HALF, PAD), BF16)
        hpad[e, :, 0:PAD] = jnp.zeros((units, PAD), BF16)
        hpad[e, :, PAD + NXY:] = jnp.zeros((units, PAD), BF16)
    far_inside = jnp.where(core == 0, z >= 2, z < n_slab - 2)
    for a in range(5):
        patches[a * SPAN + TAPS:(a + 1) * SPAN, :] = jnp.ones((EXTRA, NXY), BF16)
    for a in (0, 1, 3):

        @pl.when(jnp.logical_not(far_inside if a == 0 else inside(a - 2)))
        def _():
            whole[a] = jnp.zeros((C, NXY), BF16)
            cgot[a] = jnp.zeros((n_chan, 2 * share, NXY // 2), BF16)
            if a > 0:
                precv[a - 1] = jnp.zeros((n_chan, 2 * share, NXY), BF16)
    for one in load_small:
        one.wait()
    b2_rows[0] = jnp.broadcast_to(b2_in[1:2, :].astype(F32), (16, units)).astype(BF16)
    lone = lax.broadcasted_iota(jnp.int32, (EXTRA, units), 0) == 0
    for k in range(STEPS):
        bias = jnp.where(lone, b1_in[k:k + 1, :].astype(F32), 0.0).astype(BF16)
        for a in range(3):
            extra = slice(a * SPAN + TAPS, (a + 1) * SPAN)
            wf[k, c, extra, :] = bias if a == 1 else jnp.zeros_like(bias)
            if k == 0:
                blank = slice(extra.start + (16 if a == 1 else 0), extra.stop)
                for j in (1, 2, 3):
                    wf[0, place_of[j], blank, :] = jnp.zeros((blank.stop - blank.start, units), BF16)

    def rows_of(place):
        at = 2 * lax.rem(place, 2) + lax.div(place, 2)
        return pl.ds(pl.multiple_of(at * own, own), own)
    mine = rows_of(c)
    theirs = rows_of(place_of[2])
    pair = pl.ds(pl.multiple_of(lax.rem(c, 2) * 2 * own, 2 * own), 2 * own)
    other_pair = pl.ds(pl.multiple_of((1 - lax.rem(c, 2)) * 2 * own, 2 * own), 2 * own)
    load_field.wait()
    whole[2, mine, :] = field_in[...].astype(BF16)
    for one in load_first:
        one.wait()
    greeted = n_chan - 1
    for dz in (-1, 1):
        greeted = greeted + jnp.where(inside(dz), 1, 0)
    pl.semaphore_wait(barrier, greeted)

    def send_field(dz, js):
        send('field', dz, js, lambda j: whole.at[2, mine, :], whole.at[2 - dz, mine, :])

    def span(k, place, a):
        rows = SPAN if k == 1 else TAPS + 16 if a == 1 else TAPS
        return wf.at[k, place, pl.ds(a * SPAN, rows), :]

    def send_first(k, a, j):
        send(('first', k, a), 0, (j,), lambda j: span(k, c, a), span(k, c, a))

    def relay_first(k, a):
        arrive(('first', k, a), 0, 2, span(k, place_of[2], a))
        part = span(k, place_of[2], a)
        send(('first relay', k, a), 0, (1,), lambda j: part, part)

    def first_direct(k):
        for a in range(3):
            arrive(('first', k, a), 0, 1, span(k, place_of[1], a))

    def first_relayed(k):
        for a in range(3):
            arrive(('first relay', k, a), 0, 1, span(k, place_of[3], a))
    send_field(0, (2,))
    for a in range(3):
        send_first(0, a, 2)
    for dz in (-1, 1):
        send_field(dz, (0,))
    send_field(0, (1,))
    for a in range(3):
        send_first(0, a, 1)
    load_next = [load(w_first.at[1, a], wf.at[1, c, pl.ds(a * SPAN, TAPS), :]) for a in range(3)]
    load_rest = [load(w_middle, wm.at[0:STEPS])]
    for a in range(3):
        for b in range(3):
            load_rest.append(load(w_last.at[1, a, b], wl_next.at[0, a, :, pl.ds(b * C, C), :]))
    for a in range(3):
        load_rest.append(load(w_last.at[0, a], wl.at[:, :, pl.ds(a * C, C), :]))

    def from_columns(a):
        part = whole.at[a, theirs if a == 2 else pair, :]
        if a == 2:
            arrive('field', 0, 2, part)
            for dz in (-1, 1):
                send('field pass', dz, (0,), lambda j: part, whole.at[2 - dz, theirs, :])
        elif a in (1, 3):
            arrive('field', 2 - a, 0, whole.at[a, mine, :])
            arrive('field pass', 2 - a, 0, whole.at[a, theirs, :])
        tag = ('field relay', a)
        relay = copy(tag, 0, 1, part, part)
        when_side(a - 2, relay.start)
        started.append((a - 2, relay))

    def from_core(a):
        if a == 2:
            arrive('field', 0, 1, whole.at[2, rows_of(place_of[1]), :])
            part = whole.at[2, rows_of(place_of[3]), :]
        else:
            part = whole.at[a, other_pair, :]
        i = slot(('field relay', a), 0, 1)

        def wait():
            pltpu.make_async_remote_copy(src_ref=part, dst_ref=part, send_sem=send_sem.at[i], recv_sem=recv_sem.at[i], device_id=peer(0, 1), device_id_type=MESH).wait_recv()
        when_side(a - 2, wait)
    line = lax.broadcasted_iota(jnp.int32, (C, C), 0)

    def hits(k, channel):
        return (channel == order_in[k:k + 1, :]).astype(F32).T.astype(BF16)
    block = lax.div(line, own)
    perm[0] = hits(0, (2 * lax.rem(block, 2) + lax.div(block, 2)) * own + lax.rem(line, own))
    perm[1] = hits(1, line)
    sent = HALF + lax.div(line, 2 * share) * share + lax.rem(line, share)
    low = lax.rem(lax.div(line, share), 2) == 0
    perm[2] = hits(1, jnp.where(low, sent, -1))
    perm[3] = hits(1, jnp.where(low, -1, sent))
    for k in range(STEPS):
        bias2[k] = jnp.broadcast_to(b2_in[k:k + 1, :].astype(F32), (128, units)).T
        bias3[k] = jnp.broadcast_to(b3_in[k:k + 1, :].astype(F32), (128, C)).T
    y = lax.rem(lax.broadcasted_iota(jnp.int32, (1, NXY), 1), NY)
    lane = lax.broadcasted_iota(jnp.int32, (1, NXY), 1)

    def keep(values, e):
        if e == 0:
            return jnp.where(y == NY - 1, 0.0, values)
        if e == 2:
            return jnp.where(y == 0, 0.0, values)
        return values

    def shifted(b, e):
        start = PAD + NY * (b - 1) + (e - 1)
        return slice(start, start + NXY)

    def wide(column):
        return jnp.concatenate([column.astype(F32)] * (NXY // 128), axis=1)

    def lay(a, front, base=None):
        base = a * SPAN if base is None else base
        for e in range(3):
            xpad[e, a * HALF:(a + 1) * HALF, PAD:PAD + NXY] = keep(front, e).astype(BF16)
        for b in range(3):
            for e in range(3):
                at = base + (b * 3 + e) * HALF
                if not isinstance(at, int):
                    at = pl.multiple_of(at, HALF)
                patches[pl.ds(at, HALF), :] = xpad[e, a * HALF:(a + 1) * HALF, shifted(b, e)]

    def convolve(k, place, p, base=None):
        rows = place * units if isinstance(place, int) else pl.multiple_of(place * units, units)
        one = lax.dot_general(wf[k, place], patches[pl.ds(p * SPAN if base is None else base, 3 * SPAN), :], (((0,), (0,)), ((), ())), preferred_element_type=F32)
        hidden[p, pl.ds(rows, units), :] = jnp.maximum(one, 0.0).astype(BF16)

    def finish():
        for wanted, one in far_started:
            pl.when(wanted)(one.wait_send)
        for dz, one in started:
            when_side(dz, one.wait_send)
    from_columns(2)
    for one in load_next:
        one.wait()
    relay_first(0, 0)
    for a in range(3):
        send_first(1, a, 2)
    for a in (1, 3):
        from_columns(a)
    relay_first(0, 1)
    relay_first(0, 2)
    for a in (2, 1, 3):
        from_core(a)
        if a == 2:
            permuted = jnp.dot(perm[0], whole[2], preferred_element_type=F32)
            back[...] = permuted
            front = permuted[:HALF]
        else:
            front = jnp.dot(perm[0, 0:HALF, :], whole[a], preferred_element_type=F32)
        fronts[a] = front.astype(BF16)
        lay(a, front)
    send_far('pair', (0,), (1,), whole.at[2, pair, :], whole.at[0, pair, :])
    convolve(0, c, 1)
    first_direct(0)
    convolve(0, place_of[1], 1)
    convolve(0, place_of[2], 1)
    first_relayed(0)
    convolve(0, place_of[3], 1)
    for one in load_rest:
        one.wait()
    summed = jnp.dot(wm[0], hidden[1], preferred_element_type=F32)
    two = jnp.maximum(summed + wide(bias2[0]), 0.0)
    for e in range(3):
        hpad[e, :, PAD:PAD + NXY] = keep(two, e).astype(BF16)
    for b in range(3):
        for e in range(3):
            at = (b * 3 + e) * units
            patches3[at:at + units, :] = hpad[e, :, shifted(b, e)]
    weights = jnp.concatenate([wl[b, e] for b in range(3) for e in range(3)], axis=1)
    parts = jnp.dot(weights, patches3[...], preferred_element_type=F32)
    for s in range(n_chan):
        for a in range(3):
            at = a * C + s * share
            psend[s, a] = jnp.concatenate([parts[at:at + share], parts[at + HALF:at + HALF + share]], axis=0).astype(BF16)
    for dz in (-1, 1):
        send('parts', dz, (2, 3, 1, 0), lambda j: psend.at[place_of[j], 1 - dz], precv.at[1 - dz, c])
    send('parts', 0, (2, 3, 1), lambda j: psend.at[place_of[j], 1], precv.at[1, c])
    precv[1, c] = psend[c, 1]
    for a in range(3):
        relay_first(1, a)
    for a in range(3):
        send_first(1, a, 1)
    send('bias', 0, (1,), lambda j: b2_rows.at[0], b2_rows.at[1])
    send('middle', 0, (1,), lambda j: wm.at[1], wm.at[2])
    send('last', 0, (1,), lambda j: wl_next.at[0], wl_next.at[1])
    for j in (1, 2, 3):
        arrive('parts', 0, j, precv.at[1, place_of[j]])
    total = precv[1, 0].astype(F32)
    for s in range(1, n_chan):
        total = total + precv[1, s].astype(F32)
    for a in (0, 2):
        for j in range(n_chan):
            arrive('parts', 1 - a, j, precv.at[a, place_of[j]])
    for a in (0, 2):
        for s in range(n_chan):
            total = total + precv[a, s].astype(F32)
    scales = pl.ds(pl.multiple_of(c * share, share), share)
    shifts = pl.ds(pl.multiple_of(HALF + c * share, share), share)
    arg = total[:share] + wide(bias3[0, scales, :]) + 2.0
    coupled = (back[shifts, :] + total[share:] + wide(bias3[0, shifts, :])) * jax.nn.sigmoid(arg)
    packed = jnp.concatenate([coupled[:, :NXY // 2], coupled[:, NXY // 2:]], axis=0)
    csend[...] = packed.astype(BF16)
    send_far('coupled', (2, 0), (3, 1), csend, cgot.at[0, c])
    for dz in (-1, 1):
        send('coupled', dz, (3, 2, 0, 1), lambda j: csend, cgot.at[2 - dz, c])
    send('coupled', 0, (3, 2, 1), lambda j: csend, cgot.at[2, c])
    cgot[2, c] = packed.astype(BF16)

    def log_means(k, arg):
        soft = jnp.minimum(arg, 0.0) - jnp.log1p(jnp.exp(-jnp.abs(arg)))
        means = jnp.broadcast_to(jnp.sum(soft, axis=1, keepdims=True) * (1.0 / NXY), (share, share))
        diagonal = lax.broadcasted_iota(jnp.int32, (share, share), 0) == lax.broadcasted_iota(jnp.int32, (share, share), 1)
        logscale[k] = jnp.sum(jnp.where(diagonal, means, 0.0), axis=0, keepdims=True)
    log_means(0, arg)
    far_arrives('pair', 0, whole.at[0, pair, :])
    far_arrives('pair', 1, whole.at[0, other_pair, :])
    front = jnp.dot(perm[0, 0:HALF, :], whole[0], preferred_element_type=F32)
    fronts[0] = front.astype(BF16)
    arrive('bias', 0, 1, b2_rows.at[1])
    bias2[2] = jnp.broadcast_to(b2_rows[1, 0:1, :].astype(F32), (128, units)).T
    arrive('middle', 0, 1, wm.at[2])
    arrive('last', 0, 1, wl_next.at[1])
    first_direct(1)
    first_relayed(1)

    def front_of(a, rows):
        kept = jnp.dot(perm[1, 0:rows, 0:HALF], fronts[a], preferred_element_type=F32)
        got = jnp.concatenate([cgot[a, s] for s in range(n_chan)], axis=0)
        halves = [jnp.dot(perm[i, 0:rows, :], got, preferred_element_type=F32) for i in (2, 3)]
        return kept + jnp.concatenate(halves, axis=1)

    def coupled_arrives(a):
        if a == 0:
            for j in (1, 2, 3, 0):
                far_arrives('coupled', j, cgot.at[0, place_of[j]])
            return
        for j in (1, 2, 3, 0):
            if (a, j) != (2, 0):
                arrive('coupled', 2 - a, j, cgot.at[a, place_of[j]])
    for a in (2, 1, 3):
        coupled_arrives(a)
        if a == 2:
            permuted = front_of(2, C)
            back[...] = permuted
            front = permuted[:HALF]
        else:
            front = front_of(a, HALF)
        lay(a, front)
    for s in range(n_chan):
        convolve(1, s, 1)
    coupled_arrives(0)
    lay(0, front_of(0, HALF), core * 4 * SPAN)
    for s in range(n_chan):
        convolve(1, s, 0, pl.multiple_of(core * 2 * SPAN, 2 * SPAN))

    def keep_two(two, at):
        left = jnp.where(y == 0, 0.0, pltpu.roll(two, 1, 1))
        right = jnp.where(y == NY - 1, 0.0, pltpu.roll(two, NXY - 1, 1))
        for e, values in enumerate((left, two, right)):
            rows = two.shape[0]
            patches3[at + e * rows:at + (e + 1) * rows, :] = values.astype(BF16)
    two = jnp.dot(wm[1], hidden[1], preferred_element_type=F32) + wide(bias2[1])
    keep_two(jnp.maximum(two, 0.0), 0)
    bias = jnp.concatenate([wide(bias2[1]), wide(bias2[2])], axis=0)
    middle = jnp.concatenate([wm[1], wm[2]], axis=0)
    two = jnp.maximum(jnp.dot(middle, hidden[0], preferred_element_type=F32) + bias, 0.0)
    beside = jnp.where(core == 0, z > 0, z < n_slab - 1)
    keep_two(jnp.where(beside, two, 0.0), 3 * units)
    weights = jnp.concatenate([wl_next[0, 1, e] for e in range(3)] + [wl_next[i, 2 * core, e] for e in range(3) for i in range(2)], axis=1)
    parts = jnp.dot(weights, patches3[...], preferred_element_type=F32)
    part = parts[C:2 * C]
    part = part + jnp.where(lane < NY, 0.0, pltpu.roll(parts[0:C], NY, 1))
    part = part + jnp.where(lane >= NXY - NY, 0.0, pltpu.roll(parts[2 * C:], NXY - NY, 1))
    for i in range(2):
        at = i * own
        net_send[i] = jnp.concatenate([part[at:at + own], part[HALF + at:HALF + at + own]], axis=0).astype(BF16)
    for s in range(n_chan):
        rows = part[s * share:(s + 1) * share]
        scale_send[s] = jnp.concatenate([rows[:, :NXY // 2], rows[:, NXY // 2:]], axis=0).astype(BF16)
    nets = []
    for j in (3, 2, 1):
        to = place_of[j]
        one = copy('net', 0, j, net_send.at[lax.rem(to, 2)], net_recv.at[j])
        nets.append((to, one))
        pl.when(to >= n_chan // 2)(one.start)
        send('scale', 0, (j,), lambda j: scale_send.at[place_of[j]], scale_recv.at[j])
    net[...] = part + wide(bias3[1])
    kept = pl.ds(pl.multiple_of(lax.rem(c, 2) * own, own), own)
    moved = pl.ds(pl.multiple_of(HALF + lax.rem(c, 2) * own, own), own)

    @pl.when(c < n_chan // 2)
    def _():
        flowed[...] = back[kept, :]

    @pl.when(c >= n_chan // 2)
    def _():
        scaled, added = (net[kept, :], net[moved, :])
        for j in (1, 2, 3):
            arrive('net', 0, j, net_recv.at[j])
            got = net_recv[j].astype(F32)
            scaled, added = (scaled + got[:own], added + got[own:])
        flowed[...] = (back[moved, :] + added) * jax.nn.sigmoid(scaled + 2.0)
    arg = net[scales, :] + 2.0
    for j in (1, 2, 3):
        arrive('scale', 0, j, scale_recv.at[j])
        got = scale_recv[j].astype(F32)
        arg = arg + jnp.concatenate([got[:share], got[share:]], axis=1)
    log_means(1, arg)
    for to, one in nets:
        pl.when(to >= n_chan // 2)(one.wait_send)
    finish()


def store(moved, means, flowed, logscale):
    flowed[:, 0, :] = moved[...]
    logscale[...] = means[...]


def local(field, order, w_first, b_first, w_middle, b_middle, w_last, b_last):
    n_chan = lax.axis_size('chan')
    share = HALF // n_chan
    own = C // n_chan
    units = w_first.shape[1]
    vmem = pl.BlockSpec(memory_space=pltpu.VMEM)
    hbm = pl.BlockSpec(memory_space=pl.ANY)
    moved, means = pl.pallas_call(kernel, out_shape=(pltpu.VMEM((own, NXY), F32), pltpu.VMEM((STEPS, 1, share), F32)), in_specs=[hbm] * 8, out_specs=(vmem, vmem), scratch_shapes=[pltpu.VMEM((own, NXY), F32), pltpu.VMEM(order.shape, jnp.int32), pltpu.VMEM(b_first.shape, BF16), pltpu.VMEM(b_middle.shape, BF16), pltpu.VMEM(b_last.shape, BF16), pltpu.VMEM((STEPS, n_chan, 3 * SPAN, units), BF16), pltpu.VMEM((STEPS + 1, units, n_chan * units), BF16), pltpu.VMEM((3, 3, 3 * C, units), BF16), pltpu.VMEM((2, 3, 3, 3 * C, units), BF16), pltpu.VMEM((STEPS + 1, units, 128), F32), pltpu.VMEM((STEPS, C, 128), F32), pltpu.VMEM((4, C, C), BF16), pltpu.VMEM((4, C, NXY), BF16), pltpu.VMEM((3, 5 * HALF, NXY + 2 * PAD), BF16), pltpu.VMEM((5 * SPAN, NXY), BF16), pltpu.VMEM((2, n_chan * units, NXY), BF16), pltpu.VMEM((3, units, NXY + 2 * PAD), BF16), pltpu.VMEM((9 * units, NXY), BF16), pltpu.VMEM((n_chan, 3, 2 * share, NXY), BF16), pltpu.VMEM((3, n_chan, 2 * share, NXY), BF16), pltpu.VMEM((C, NXY), F32), pltpu.VMEM((2 * share, NXY // 2), BF16), pltpu.VMEM((4, n_chan, 2 * share, NXY // 2), BF16), pltpu.VMEM((4, HALF, NXY), BF16), pltpu.VMEM((2, 2 * own, NXY), BF16), pltpu.VMEM((n_chan, 2 * own, NXY), BF16), pltpu.VMEM((n_chan, 2 * share, NXY // 2), BF16), pltpu.VMEM((n_chan, 2 * share, NXY // 2), BF16), pltpu.VMEM((C, NXY), F32), pltpu.VMEM((2, 16, units), BF16), pltpu.SemaphoreType.DMA((32,)), pltpu.SemaphoreType.DMA((SEMS,)), pltpu.SemaphoreType.DMA((SEMS,))], compiler_params=pltpu.CompilerParams(collective_id=0, has_side_effects=True, vmem_limit_bytes=62 << 20))(field, order, jnp.swapaxes(w_first, 1, 2).reshape(STEPS, 3, TAPS, units), b_first, w_middle, b_middle, w_last.reshape(STEPS, 3, 3, 3, C, units), b_last)
    moved, means = (pltpu.with_memory_space_constraint(v, pltpu.VMEM) for v in (moved, means))
    flowed, logscale = pl.pallas_call(store, out_shape=(jax.ShapeDtypeStruct(field.shape, F32), jax.ShapeDtypeStruct((STEPS, 1, share), F32)), in_specs=[vmem, vmem], out_specs=(vmem, vmem))(moved, means)
    return (flowed, jnp.swapaxes(logscale, 1, 2))


def solution(mesh):
    return jax.shard_map(local, mesh=mesh, in_specs=(P('chan', ('groups', 'slab'), None), P(), P(None, 'chan', None), P(None, 'chan'), P(None, 'chan', None), P(None, 'chan'), P(None, None, 'chan'), P()), out_specs=(P('chan', ('groups', 'slab'), None), P(None, 'chan', ('groups', 'slab'))), check_vma=False)
```

```python
import jax
import jax.numpy as jnp
from jax import lax
from jax.experimental import pallas as pl
from jax.experimental.pallas import tpu as pltpu
from jax.sharding import PartitionSpec as P
C = 64
HALF = 32
STEPS = 2
NY = 64
NXY = 512
PAD = 128
TAPS = 9 * HALF
EXTRA = 32
SPAN = TAPS + EXTRA
SEMS = 96
MESH = pl.DeviceIdType.MESH
F32 = jnp.float32
BF16 = jnp.bfloat16


def kernel(field, order, w_first, b_first, w_middle, b_middle, w_last, b_last, flowed, logscale, field_in, order_in, b1_in, b2_in, b3_in, wf, wm, wl, wl_next, bias2, bias3, perm, whole, xpad, patches, hidden, hpad, patches3, psend, precv, back, csend, cgot, fronts, net_send, net_recv, scale_send, scale_recv, net, b2_rows, load_sem, send_sem, recv_sem):
    n_chan = lax.axis_size('chan')
    assert n_chan == 4
    n_slab = lax.axis_size('slab')
    assert lax.axis_size('groups') == 2
    g = lax.axis_index('groups')
    twin = {'groups': 1 - g}
    c = lax.axis_index('chan')
    z = lax.axis_index('slab')
    share = HALF // n_chan
    own = C // n_chan
    units = wf.shape[3]
    place_of = (c, c + 1 - 2 * lax.rem(c, 2), lax.rem(c + 2, 4), 3 - c)
    slots = {}
    started = []

    def slot(*key):
        index = slots.setdefault(key, len(slots))
        assert index < SEMS
        return index

    def peer(dz, j):
        return {'slab': z + dz, 'chan': place_of[j]}

    def inside(dz):
        return z >= -dz if dz < 0 else z < n_slab - dz

    def when_side(dz, fn):
        if dz == 0:
            fn()
        else:
            pl.when(inside(dz))(fn)

    def copy(tag, dz, j, src, dst):
        i = slot(tag, dz, j)
        return pltpu.make_async_remote_copy(src_ref=src, dst_ref=dst, send_sem=send_sem.at[i], recv_sem=recv_sem.at[i], device_id=peer(dz, j), device_id_type=MESH)

    def send(tag, dz, js, src, dst):
        copies = [copy(tag, dz, j, src(j), dst) for j in js]

        def go():
            for one in copies:
                one.start()
        when_side(dz, go)
        started.extend(((dz, one) for one in copies))

    def arrive(tag, dz, j, dst):
        i = slot(tag, dz, j)

        def wait():
            pltpu.make_async_remote_copy(src_ref=dst, dst_ref=dst, send_sem=send_sem.at[i], recv_sem=recv_sem.at[i], device_id=peer(0, 1), device_id_type=MESH).wait_recv()
        when_side(-dz, wait)
    barrier = pltpu.get_barrier_semaphore()

    def greet(device):
        pl.semaphore_signal(barrier, inc=1, device_id=device, device_id_type=MESH)
    for dz in (-1, 1):
        when_side(dz, lambda dz=dz: greet(peer(dz, 0)))
    for j in (3, 2, 1):
        greet(peer(0, j))
    greet(twin)
    far_started = []

    def send_far(tag, same, other, src, dst):
        for dz in (-2, 2):
            for js, mine_too in ((same, True), (other, False)):
                copies = [copy(tag, dz, j, src, dst) for j in js]
                wanted = jnp.logical_and(inside(dz), core == (0 if (dz == 2) == mine_too else 1))

                @pl.when(wanted)
                def _():
                    for one in copies:
                        one.start()
                far_started.extend(((wanted, one) for one in copies))

    def far_arrives(tag, j, dst):
        for dz in (-2, 2):
            i = slot(tag, dz, j)

            @pl.when(jnp.logical_and(inside(-dz), core == (0 if dz == 2 else 1)))
            def _():
                pltpu.make_async_remote_copy(src_ref=dst, dst_ref=dst, send_sem=send_sem.at[i], recv_sem=recv_sem.at[i], device_id=peer(0, 1), device_id_type=MESH).wait_recv()
    core = lax.rem(c, 2)
    loads = []

    def load(src, dst):
        one = pltpu.make_async_copy(src, dst, load_sem.at[len(loads)])
        one.start()
        loads.append(one)
        return one
    load_field = load(field.at[:, 0, :], field_in)
    load_first = [load(w_first.at[0, a], wf.at[0, c, pl.ds(a * SPAN, TAPS), :]) for a in range(3)]
    load_small = [load(order, order_in), load(b_first, b1_in), load(b_middle, b2_in), load(b_last, b3_in)]
    for e in range(3):
        xpad[e, :, 0:PAD] = jnp.zeros((5 * HALF, PAD), BF16)
        xpad[e, :, PAD + NXY:] = jnp.zeros((5 * HALF, PAD), BF16)
        hpad[e, :, 0:PAD] = jnp.zeros((units, PAD), BF16)
        hpad[e, :, PAD + NXY:] = jnp.zeros((units, PAD), BF16)
    far_inside = jnp.where(core == 0, z >= 2, z < n_slab - 2)
    for a in range(5):
        patches[a * SPAN + TAPS:(a + 1) * SPAN, :] = jnp.ones((EXTRA, NXY), BF16)
    for a in (0, 1, 3):

        @pl.when(jnp.logical_not(far_inside if a == 0 else inside(a - 2)))
        def _():
            whole[a] = jnp.zeros((C, NXY), BF16)
            cgot[a] = jnp.zeros((n_chan, 2 * share, NXY // 2), BF16)
            if a > 0:
                precv[a - 1] = jnp.zeros((n_chan, 2 * share, NXY), BF16)
    for one in load_small:
        one.wait()
    b2_rows[0] = jnp.broadcast_to(b2_in[1:2, :].astype(F32), (16, units)).astype(BF16)
    lone = lax.broadcasted_iota(jnp.int32, (EXTRA, units), 0) == 0
    for k in range(STEPS):
        bias = jnp.where(lone, b1_in[k:k + 1, :].astype(F32), 0.0).astype(BF16)
        for a in range(3):
            extra = slice(a * SPAN + TAPS, (a + 1) * SPAN)
            wf[k, c, extra, :] = bias if a == 1 else jnp.zeros_like(bias)
            if k == 0:
                blank = slice(extra.start + (16 if a == 1 else 0), extra.stop)
                for j in (1, 2, 3):
                    wf[0, place_of[j], blank, :] = jnp.zeros((blank.stop - blank.start, units), BF16)

    def rows_of(place):
        at = 2 * lax.rem(place, 2) + lax.div(place, 2)
        return pl.ds(pl.multiple_of(at * own, own), own)
    mine = rows_of(c)
    theirs = rows_of(place_of[2])
    pair = pl.ds(pl.multiple_of(lax.rem(c, 2) * 2 * own, 2 * own), 2 * own)
    other_pair = pl.ds(pl.multiple_of((1 - lax.rem(c, 2)) * 2 * own, 2 * own), 2 * own)
    load_field.wait()
    whole[2, mine, :] = field_in[...].astype(BF16)
    for one in load_first:
        one.wait()
    greeted = n_chan
    for dz in (-1, 1):
        greeted = greeted + jnp.where(inside(dz), 1, 0)
    pl.semaphore_wait(barrier, greeted)

    def send_field(dz, js):
        send('field', dz, js, lambda j: whole.at[2, mine, :], whole.at[2 - dz, mine, :])

    def span(k, place, a):
        rows = SPAN if k == 1 else TAPS + 16 if a == 1 else TAPS
        return wf.at[k, place, pl.ds(a * SPAN, rows), :]

    def send_first(k, a, j):
        send(('first', k, a), 0, (j,), lambda j: span(k, c, a), span(k, c, a))

    def relay_first(k, a):
        arrive(('first', k, a), 0, 2, span(k, place_of[2], a))
        part = span(k, place_of[2], a)
        send(('first relay', k, a), 0, (1,), lambda j: part, part)

    def half(place, side):
        rows = 3 * SPAN // 2
        return wf.at[1, place, pl.ds(pl.multiple_of(side * rows, rows), rows), :]

    def twin_copy():
        i = slot('twin')
        part = half(place_of[2], g)
        return pltpu.make_async_remote_copy(src_ref=part, dst_ref=part, send_sem=send_sem.at[i], recv_sem=recv_sem.at[i], device_id=twin, device_id_type=MESH)

    def twin_arrives():
        i = slot('twin')
        part = half(place_of[2], 1 - g)
        pltpu.make_async_remote_copy(src_ref=part, dst_ref=part, send_sem=send_sem.at[i], recv_sem=recv_sem.at[i], device_id=twin, device_id_type=MESH).wait_recv()

    def relay_half(i, side):
        part = half(place_of[2], side)
        send(('half relay', i), 0, (1,), lambda j: part, part)

    def first_direct(k):
        for a in range(3):
            arrive(('first', k, a), 0, 1, span(k, place_of[1], a))

    def first_relayed(k):
        for a in range(3):
            arrive(('first relay', k, a), 0, 1, span(k, place_of[3], a))
    send_field(0, (2,))
    for a in range(3):
        send_first(0, a, 2)
    for dz in (-1, 1):
        send_field(dz, (0,))
    send_field(0, (1,))
    for a in range(3):
        send_first(0, a, 1)
    load_next = [load(w_first.at[1, a], wf.at[1, c, pl.ds(a * SPAN, TAPS), :]) for a in range(3)]
    load_rest = [load(w_middle, wm.at[0:STEPS])]
    for a in range(3):
        for b in range(3):
            load_rest.append(load(w_last.at[1, a, b], wl_next.at[0, a, :, pl.ds(b * C, C), :]))
    for a in range(3):
        load_rest.append(load(w_last.at[0, a], wl.at[:, :, pl.ds(a * C, C), :]))

    def from_columns(a):
        part = whole.at[a, theirs if a == 2 else pair, :]
        if a == 2:
            arrive('field', 0, 2, part)
            for dz in (-1, 1):
                send('field pass', dz, (0,), lambda j: part, whole.at[2 - dz, theirs, :])
        elif a in (1, 3):
            arrive('field', 2 - a, 0, whole.at[a, mine, :])
            arrive('field pass', 2 - a, 0, whole.at[a, theirs, :])
        tag = ('field relay', a)
        relay = copy(tag, 0, 1, part, part)
        when_side(a - 2, relay.start)
        started.append((a - 2, relay))

    def from_core(a):
        if a == 2:
            arrive('field', 0, 1, whole.at[2, rows_of(place_of[1]), :])
            part = whole.at[2, rows_of(place_of[3]), :]
        else:
            part = whole.at[a, other_pair, :]
        i = slot(('field relay', a), 0, 1)

        def wait():
            pltpu.make_async_remote_copy(src_ref=part, dst_ref=part, send_sem=send_sem.at[i], recv_sem=recv_sem.at[i], device_id=peer(0, 1), device_id_type=MESH).wait_recv()
        when_side(a - 2, wait)
    line = lax.broadcasted_iota(jnp.int32, (C, C), 0)

    def hits(k, channel):
        return (channel == order_in[k:k + 1, :]).astype(F32).T.astype(BF16)
    block = lax.div(line, own)
    perm[0] = hits(0, (2 * lax.rem(block, 2) + lax.div(block, 2)) * own + lax.rem(line, own))
    perm[1] = hits(1, line)
    sent = HALF + lax.div(line, 2 * share) * share + lax.rem(line, share)
    low = lax.rem(lax.div(line, share), 2) == 0
    perm[2] = hits(1, jnp.where(low, sent, -1))
    perm[3] = hits(1, jnp.where(low, -1, sent))
    for k in range(STEPS):
        bias2[k] = jnp.broadcast_to(b2_in[k:k + 1, :].astype(F32), (128, units)).T
        bias3[k] = jnp.broadcast_to(b3_in[k:k + 1, :].astype(F32), (128, C)).T
    y = lax.rem(lax.broadcasted_iota(jnp.int32, (1, NXY), 1), NY)
    lane = lax.broadcasted_iota(jnp.int32, (1, NXY), 1)

    def keep(values, e):
        if e == 0:
            return jnp.where(y == NY - 1, 0.0, values)
        if e == 2:
            return jnp.where(y == 0, 0.0, values)
        return values

    def shifted(b, e):
        start = PAD + NY * (b - 1) + (e - 1)
        return slice(start, start + NXY)

    def wide(column):
        return jnp.concatenate([column.astype(F32)] * (NXY // 128), axis=1)

    def lay(a, front, base=None):
        base = a * SPAN if base is None else base
        for e in range(3):
            xpad[e, a * HALF:(a + 1) * HALF, PAD:PAD + NXY] = keep(front, e).astype(BF16)
        for b in range(3):
            for e in range(3):
                at = base + (b * 3 + e) * HALF
                if not isinstance(at, int):
                    at = pl.multiple_of(at, HALF)
                patches[pl.ds(at, HALF), :] = xpad[e, a * HALF:(a + 1) * HALF, shifted(b, e)]

    def convolve(k, place, p, base=None):
        rows = place * units if isinstance(place, int) else pl.multiple_of(place * units, units)
        one = lax.dot_general(wf[k, place], patches[pl.ds(p * SPAN if base is None else base, 3 * SPAN), :], (((0,), (0,)), ((), ())), preferred_element_type=F32)
        hidden[p, pl.ds(rows, units), :] = jnp.maximum(one, 0.0).astype(BF16)

    def finish():
        for wanted, one in far_started:
            pl.when(wanted)(one.wait_send)
        for dz, one in started:
            when_side(dz, one.wait_send)
    from_columns(2)
    for one in load_next:
        one.wait()
    relay_first(0, 0)
    for a in (1, 3):
        from_columns(a)
    relay_first(0, 1)
    relay_first(0, 2)
    send('half', 0, (2,), lambda j: half(c, g), half(c, g))
    for a in (2, 1, 3):
        from_core(a)
        if a == 2:
            permuted = jnp.dot(perm[0], whole[2], preferred_element_type=F32)
            back[...] = permuted
            front = permuted[:HALF]
        else:
            front = jnp.dot(perm[0, 0:HALF, :], whole[a], preferred_element_type=F32)
        fronts[a] = front.astype(BF16)
        lay(a, front)
    send_far('pair', (0,), (1,), whole.at[2, pair, :], whole.at[0, pair, :])
    convolve(0, c, 1)
    first_direct(0)
    convolve(0, place_of[1], 1)
    convolve(0, place_of[2], 1)
    first_relayed(0)
    convolve(0, place_of[3], 1)
    for one in load_rest:
        one.wait()
    summed = jnp.dot(wm[0], hidden[1], preferred_element_type=F32)
    two = jnp.maximum(summed + wide(bias2[0]), 0.0)
    for e in range(3):
        hpad[e, :, PAD:PAD + NXY] = keep(two, e).astype(BF16)
    for b in range(3):
        for e in range(3):
            at = (b * 3 + e) * units
            patches3[at:at + units, :] = hpad[e, :, shifted(b, e)]
    weights = jnp.concatenate([wl[b, e] for b in range(3) for e in range(3)], axis=1)
    parts = jnp.dot(weights, patches3[...], preferred_element_type=F32)
    for s in range(n_chan):
        for a in range(3):
            at = a * C + s * share
            psend[s, a] = jnp.concatenate([parts[at:at + share], parts[at + HALF:at + HALF + share]], axis=0).astype(BF16)
    for dz in (-1, 1):
        send('parts', dz, (2, 3, 1, 0), lambda j: psend.at[place_of[j], 1 - dz], precv.at[1 - dz, c])
    send('parts', 0, (2, 3, 1), lambda j: psend.at[place_of[j], 1], precv.at[1, c])
    precv[1, c] = psend[c, 1]
    arrive('half', 0, 2, half(place_of[2], g))
    one = twin_copy()
    one.start()
    started.append((0, one))
    relay_half(0, g)
    for a in range(3):
        send_first(1, a, 1)
    send('bias', 0, (1,), lambda j: b2_rows.at[0], b2_rows.at[1])
    send('middle', 0, (1,), lambda j: wm.at[1], wm.at[2])
    send('last', 0, (1,), lambda j: wl_next.at[0], wl_next.at[1])
    for j in (1, 2, 3):
        arrive('parts', 0, j, precv.at[1, place_of[j]])
    total = precv[1, 0].astype(F32)
    for s in range(1, n_chan):
        total = total + precv[1, s].astype(F32)
    for a in (0, 2):
        for j in range(n_chan):
            arrive('parts', 1 - a, j, precv.at[a, place_of[j]])
    for a in (0, 2):
        for s in range(n_chan):
            total = total + precv[a, s].astype(F32)
    scales = pl.ds(pl.multiple_of(c * share, share), share)
    shifts = pl.ds(pl.multiple_of(HALF + c * share, share), share)
    arg = total[:share] + wide(bias3[0, scales, :]) + 2.0
    coupled = (back[shifts, :] + total[share:] + wide(bias3[0, shifts, :])) * jax.nn.sigmoid(arg)
    packed = jnp.concatenate([coupled[:, :NXY // 2], coupled[:, NXY // 2:]], axis=0)
    csend[...] = packed.astype(BF16)
    send_far('coupled', (2, 0), (3, 1), csend, cgot.at[0, c])
    for dz in (-1, 1):
        send('coupled', dz, (3, 2, 0, 1), lambda j: csend, cgot.at[2 - dz, c])
    send('coupled', 0, (3, 2, 1), lambda j: csend, cgot.at[2, c])
    cgot[2, c] = packed.astype(BF16)

    def log_means(k, arg):
        soft = jnp.minimum(arg, 0.0) - jnp.log1p(jnp.exp(-jnp.abs(arg)))
        means = jnp.broadcast_to(jnp.sum(soft, axis=1, keepdims=True) * (1.0 / NXY), (share, share))
        diagonal = lax.broadcasted_iota(jnp.int32, (share, share), 0) == lax.broadcasted_iota(jnp.int32, (share, share), 1)
        logscale[k] = jnp.sum(jnp.where(diagonal, means, 0.0), axis=0, keepdims=True)
    log_means(0, arg)
    far_arrives('pair', 0, whole.at[0, pair, :])
    far_arrives('pair', 1, whole.at[0, other_pair, :])
    front = jnp.dot(perm[0, 0:HALF, :], whole[0], preferred_element_type=F32)
    fronts[0] = front.astype(BF16)
    arrive('bias', 0, 1, b2_rows.at[1])
    bias2[2] = jnp.broadcast_to(b2_rows[1, 0:1, :].astype(F32), (128, units)).T
    arrive('middle', 0, 1, wm.at[2])
    arrive('last', 0, 1, wl_next.at[1])
    first_direct(1)
    arrive(('half relay', 0), 0, 1, half(place_of[3], g))
    twin_arrives()
    relay_half(1, 1 - g)

    def front_of(a, rows):
        kept = jnp.dot(perm[1, 0:rows, 0:HALF], fronts[a], preferred_element_type=F32)
        got = jnp.concatenate([cgot[a, s] for s in range(n_chan)], axis=0)
        halves = [jnp.dot(perm[i, 0:rows, :], got, preferred_element_type=F32) for i in (2, 3)]
        return kept + jnp.concatenate(halves, axis=1)

    def coupled_arrives(a):
        if a == 0:
            for j in (1, 2, 3, 0):
                far_arrives('coupled', j, cgot.at[0, place_of[j]])
            return
        for j in (1, 2, 3, 0):
            if (a, j) != (2, 0):
                arrive('coupled', 2 - a, j, cgot.at[a, place_of[j]])
    for a in (2, 1, 3):
        coupled_arrives(a)
        if a == 2:
            permuted = front_of(2, C)
            back[...] = permuted
            front = permuted[:HALF]
        else:
            front = front_of(a, HALF)
        lay(a, front)
    arrive(('half relay', 1), 0, 1, half(place_of[3], 1 - g))
    for s in range(n_chan):
        convolve(1, s, 1)
    coupled_arrives(0)
    lay(0, front_of(0, HALF), core * 4 * SPAN)
    for s in range(n_chan):
        convolve(1, s, 0, pl.multiple_of(core * 2 * SPAN, 2 * SPAN))

    def keep_two(two, at):
        left = jnp.where(y == 0, 0.0, pltpu.roll(two, 1, 1))
        right = jnp.where(y == NY - 1, 0.0, pltpu.roll(two, NXY - 1, 1))
        for e, values in enumerate((left, two, right)):
            rows = two.shape[0]
            patches3[at + e * rows:at + (e + 1) * rows, :] = values.astype(BF16)
    two = jnp.dot(wm[1], hidden[1], preferred_element_type=F32) + wide(bias2[1])
    keep_two(jnp.maximum(two, 0.0), 0)
    bias = jnp.concatenate([wide(bias2[1]), wide(bias2[2])], axis=0)
    middle = jnp.concatenate([wm[1], wm[2]], axis=0)
    two = jnp.maximum(jnp.dot(middle, hidden[0], preferred_element_type=F32) + bias, 0.0)
    beside = jnp.where(core == 0, z > 0, z < n_slab - 1)
    keep_two(jnp.where(beside, two, 0.0), 3 * units)
    weights = jnp.concatenate([wl_next[0, 1, e] for e in range(3)] + [wl_next[i, 2 * core, e] for e in range(3) for i in range(2)], axis=1)
    parts = jnp.dot(weights, patches3[...], preferred_element_type=F32)
    part = parts[C:2 * C]
    part = part + jnp.where(lane < NY, 0.0, pltpu.roll(parts[0:C], NY, 1))
    part = part + jnp.where(lane >= NXY - NY, 0.0, pltpu.roll(parts[2 * C:], NXY - NY, 1))
    for i in range(2):
        at = i * own
        net_send[i] = jnp.concatenate([part[at:at + own], part[HALF + at:HALF + at + own]], axis=0).astype(BF16)
    for s in range(n_chan):
        rows = part[s * share:(s + 1) * share]
        scale_send[s] = jnp.concatenate([rows[:, :NXY // 2], rows[:, NXY // 2:]], axis=0).astype(BF16)
    nets = []
    for j in (3, 2, 1):
        to = place_of[j]
        one = copy('net', 0, j, net_send.at[lax.rem(to, 2)], net_recv.at[j])
        nets.append((to, one))
        pl.when(to >= n_chan // 2)(one.start)
        send('scale', 0, (j,), lambda j: scale_send.at[place_of[j]], scale_recv.at[j])
    net[...] = part + wide(bias3[1])
    kept = pl.ds(pl.multiple_of(lax.rem(c, 2) * own, own), own)
    moved = pl.ds(pl.multiple_of(HALF + lax.rem(c, 2) * own, own), own)

    @pl.when(c < n_chan // 2)
    def _():
        flowed[...] = back[kept, :]

    @pl.when(c >= n_chan // 2)
    def _():
        scaled, added = (net[kept, :], net[moved, :])
        for j in (1, 2, 3):
            arrive('net', 0, j, net_recv.at[j])
            got = net_recv[j].astype(F32)
            scaled, added = (scaled + got[:own], added + got[own:])
        flowed[...] = (back[moved, :] + added) * jax.nn.sigmoid(scaled + 2.0)
    arg = net[scales, :] + 2.0
    for j in (1, 2, 3):
        arrive('scale', 0, j, scale_recv.at[j])
        got = scale_recv[j].astype(F32)
        arg = arg + jnp.concatenate([got[:share], got[share:]], axis=1)
    log_means(1, arg)
    for to, one in nets:
        pl.when(to >= n_chan // 2)(one.wait_send)
    finish()


def store(moved, means, flowed, logscale):
    flowed[:, 0, :] = moved[...]
    logscale[...] = means[...]


def local(field, order, w_first, b_first, w_middle, b_middle, w_last, b_last):
    n_chan = lax.axis_size('chan')
    share = HALF // n_chan
    own = C // n_chan
    units = w_first.shape[1]
    vmem = pl.BlockSpec(memory_space=pltpu.VMEM)
    hbm = pl.BlockSpec(memory_space=pl.ANY)
    moved, means = pl.pallas_call(kernel, out_shape=(pltpu.VMEM((own, NXY), F32), pltpu.VMEM((STEPS, 1, share), F32)), in_specs=[hbm] * 8, out_specs=(vmem, vmem), scratch_shapes=[pltpu.VMEM((own, NXY), F32), pltpu.VMEM(order.shape, jnp.int32), pltpu.VMEM(b_first.shape, BF16), pltpu.VMEM(b_middle.shape, BF16), pltpu.VMEM(b_last.shape, BF16), pltpu.VMEM((STEPS, n_chan, 3 * SPAN, units), BF16), pltpu.VMEM((STEPS + 1, units, n_chan * units), BF16), pltpu.VMEM((3, 3, 3 * C, units), BF16), pltpu.VMEM((2, 3, 3, 3 * C, units), BF16), pltpu.VMEM((STEPS + 1, units, 128), F32), pltpu.VMEM((STEPS, C, 128), F32), pltpu.VMEM((4, C, C), BF16), pltpu.VMEM((4, C, NXY), BF16), pltpu.VMEM((3, 5 * HALF, NXY + 2 * PAD), BF16), pltpu.VMEM((5 * SPAN, NXY), BF16), pltpu.VMEM((2, n_chan * units, NXY), BF16), pltpu.VMEM((3, units, NXY + 2 * PAD), BF16), pltpu.VMEM((9 * units, NXY), BF16), pltpu.VMEM((n_chan, 3, 2 * share, NXY), BF16), pltpu.VMEM((3, n_chan, 2 * share, NXY), BF16), pltpu.VMEM((C, NXY), F32), pltpu.VMEM((2 * share, NXY // 2), BF16), pltpu.VMEM((4, n_chan, 2 * share, NXY // 2), BF16), pltpu.VMEM((4, HALF, NXY), BF16), pltpu.VMEM((2, 2 * own, NXY), BF16), pltpu.VMEM((n_chan, 2 * own, NXY), BF16), pltpu.VMEM((n_chan, 2 * share, NXY // 2), BF16), pltpu.VMEM((n_chan, 2 * share, NXY // 2), BF16), pltpu.VMEM((C, NXY), F32), pltpu.VMEM((2, 16, units), BF16), pltpu.SemaphoreType.DMA((32,)), pltpu.SemaphoreType.DMA((SEMS,)), pltpu.SemaphoreType.DMA((SEMS,))], compiler_params=pltpu.CompilerParams(collective_id=0, has_side_effects=True, vmem_limit_bytes=62 << 20))(field, order, jnp.swapaxes(w_first, 1, 2).reshape(STEPS, 3, TAPS, units), b_first, w_middle, b_middle, w_last.reshape(STEPS, 3, 3, 3, C, units), b_last)
    moved, means = (pltpu.with_memory_space_constraint(v, pltpu.VMEM) for v in (moved, means))
    flowed, logscale = pl.pallas_call(store, out_shape=(jax.ShapeDtypeStruct(field.shape, F32), jax.ShapeDtypeStruct((STEPS, 1, share), F32)), in_specs=[vmem, vmem], out_specs=(vmem, vmem))(moved, means)
    return (flowed, jnp.swapaxes(logscale, 1, 2))


def solution(mesh):
    return jax.shard_map(local, mesh=mesh, in_specs=(P('chan', ('groups', 'slab'), None), P(), P(None, 'chan', None), P(None, 'chan'), P(None, 'chan', None), P(None, 'chan'), P(None, None, 'chan'), P()), out_specs=(P('chan', ('groups', 'slab'), None), P(None, 'chan', ('groups', 'slab'))), check_vma=False)
```

```python
import jax
import jax.numpy as jnp
from jax import lax
from jax.experimental import pallas as pl
from jax.experimental.pallas import tpu as pltpu
from jax.sharding import PartitionSpec as P
C = 64
HALF = 32
STEPS = 2
NY = 64
NXY = 512
PAD = 128
TAPS = 9 * HALF
EXTRA = 32
SPAN = TAPS + EXTRA
SEMS = 96
MESH = pl.DeviceIdType.MESH
F32 = jnp.float32
BF16 = jnp.bfloat16


def kernel(field, order, w_first, b_first, w_middle, b_middle, w_last, b_last, flowed, logscale, field_in, order_in, b1_in, b2_in, b3_in, wf, wm, wl, wl_next, bias2, bias3, perm, whole, xpad, patches, hidden, hpad, patches3, psend, precv, back, csend, cgot, fronts, net_send, net_recv, scale_send, scale_recv, net, b2_rows, load_sem, send_sem, recv_sem):
    n_chan = lax.axis_size('chan')
    assert n_chan == 4
    n_slab = lax.axis_size('slab')
    assert lax.axis_size('groups') == 2
    g = lax.axis_index('groups')
    twin = {'groups': 1 - g}
    c = lax.axis_index('chan')
    z = lax.axis_index('slab')
    share = HALF // n_chan
    own = C // n_chan
    units = wf.shape[3]
    place_of = (c, c + 1 - 2 * lax.rem(c, 2), lax.rem(c + 2, 4), 3 - c)
    slots = {}
    started = []

    def slot(*key):
        index = slots.setdefault(key, len(slots))
        assert index < SEMS
        return index

    def peer(dz, j):
        return {'slab': z + dz, 'chan': place_of[j]}

    def inside(dz):
        return z >= -dz if dz < 0 else z < n_slab - dz

    def when_side(dz, fn):
        if dz == 0:
            fn()
        else:
            pl.when(inside(dz))(fn)

    def copy(tag, dz, j, src, dst):
        i = slot(tag, dz, j)
        return pltpu.make_async_remote_copy(src_ref=src, dst_ref=dst, send_sem=send_sem.at[i], recv_sem=recv_sem.at[i], device_id=peer(dz, j), device_id_type=MESH)

    def send(tag, dz, js, src, dst):
        copies = [copy(tag, dz, j, src(j), dst) for j in js]

        def go():
            for one in copies:
                one.start()
        when_side(dz, go)
        started.extend(((dz, one) for one in copies))

    def arrive(tag, dz, j, dst):
        i = slot(tag, dz, j)

        def wait():
            pltpu.make_async_remote_copy(src_ref=dst, dst_ref=dst, send_sem=send_sem.at[i], recv_sem=recv_sem.at[i], device_id=peer(0, 1), device_id_type=MESH).wait_recv()
        when_side(-dz, wait)
    barrier = pltpu.get_barrier_semaphore()

    def greet(device):
        pl.semaphore_signal(barrier, inc=1, device_id=device, device_id_type=MESH)
    for dz in (-1, 1):
        when_side(dz, lambda dz=dz: greet(peer(dz, 0)))
    for j in (3, 2, 1):
        greet(peer(0, j))
    greet(twin)
    far_started = []

    def send_far(tag, same, other, src, dst):
        for dz in (-2, 2):
            for js, mine_too in ((same, True), (other, False)):
                copies = [copy(tag, dz, j, src, dst) for j in js]
                wanted = jnp.logical_and(inside(dz), core == (0 if (dz == 2) == mine_too else 1))

                @pl.when(wanted)
                def _():
                    for one in copies:
                        one.start()
                far_started.extend(((wanted, one) for one in copies))

    def far_arrives(tag, j, dst):
        for dz in (-2, 2):
            i = slot(tag, dz, j)

            @pl.when(jnp.logical_and(inside(-dz), core == (0 if dz == 2 else 1)))
            def _():
                pltpu.make_async_remote_copy(src_ref=dst, dst_ref=dst, send_sem=send_sem.at[i], recv_sem=recv_sem.at[i], device_id=peer(0, 1), device_id_type=MESH).wait_recv()
    core = lax.rem(c, 2)
    loads = []

    def load(src, dst):
        one = pltpu.make_async_copy(src, dst, load_sem.at[len(loads)])
        one.start()
        loads.append(one)
        return one
    load_field = load(field.at[:, 0, :], field_in)
    load_first = [load(w_first.at[0, a], wf.at[0, c, pl.ds(a * SPAN, TAPS), :]) for a in range(3)]
    load_small = [load(order, order_in), load(b_first, b1_in), load(b_middle, b2_in), load(b_last, b3_in)]
    for e in range(3):
        xpad[e, :, 0:PAD] = jnp.zeros((5 * HALF, PAD), BF16)
        xpad[e, :, PAD + NXY:] = jnp.zeros((5 * HALF, PAD), BF16)
        hpad[e, :, 0:PAD] = jnp.zeros((units, PAD), BF16)
        hpad[e, :, PAD + NXY:] = jnp.zeros((units, PAD), BF16)
    far_inside = jnp.where(core == 0, z >= 2, z < n_slab - 2)
    for a in range(5):
        patches[a * SPAN + TAPS:(a + 1) * SPAN, :] = jnp.ones((EXTRA, NXY), BF16)
    for a in (0, 1, 3):

        @pl.when(jnp.logical_not(far_inside if a == 0 else inside(a - 2)))
        def _():
            whole[a] = jnp.zeros((C, NXY), BF16)
            cgot[a] = jnp.zeros((n_chan, 2 * share, NXY // 2), BF16)
            if a > 0:
                precv[a - 1] = jnp.zeros((n_chan, 2 * share, NXY), BF16)
    for one in load_small:
        one.wait()
    b2_rows[0] = jnp.broadcast_to(b2_in[1:2, :].astype(F32), (16, units)).astype(BF16)
    lone = lax.broadcasted_iota(jnp.int32, (EXTRA, units), 0) == 0
    for k in range(STEPS):
        bias = jnp.where(lone, b1_in[k:k + 1, :].astype(F32), 0.0).astype(BF16)
        for a in range(3):
            extra = slice(a * SPAN + TAPS, (a + 1) * SPAN)
            wf[k, c, extra, :] = bias if a == 1 else jnp.zeros_like(bias)
            if k == 0:
                blank = slice(extra.start + (16 if a == 1 else 0), extra.stop)
                for j in (1, 2, 3):
                    wf[0, place_of[j], blank, :] = jnp.zeros((blank.stop - blank.start, units), BF16)

    def rows_of(place):
        at = 2 * lax.rem(place, 2) + lax.div(place, 2)
        return pl.ds(pl.multiple_of(at * own, own), own)
    mine = rows_of(c)
    theirs = rows_of(place_of[2])
    pair = pl.ds(pl.multiple_of(lax.rem(c, 2) * 2 * own, 2 * own), 2 * own)
    other_pair = pl.ds(pl.multiple_of((1 - lax.rem(c, 2)) * 2 * own, 2 * own), 2 * own)
    load_field.wait()
    whole[2, mine, :] = field_in[...].astype(BF16)
    for one in load_first:
        one.wait()
    greeted = n_chan
    for dz in (-1, 1):
        greeted = greeted + jnp.where(inside(dz), 1, 0)
    pl.semaphore_wait(barrier, greeted)

    def send_field(dz, js):
        send('field', dz, js, lambda j: whole.at[2, mine, :], whole.at[2 - dz, mine, :])

    def span(k, place, a):
        rows = SPAN if k == 1 else TAPS + 16 if a == 1 else TAPS
        return wf.at[k, place, pl.ds(a * SPAN, rows), :]

    def send_first(k, a, j):
        send(('first', k, a), 0, (j,), lambda j: span(k, c, a), span(k, c, a))

    def relay_first(k, a):
        arrive(('first', k, a), 0, 2, span(k, place_of[2], a))
        part = span(k, place_of[2], a)
        send(('first relay', k, a), 0, (1,), lambda j: part, part)

    def half(place, side):
        rows = 3 * SPAN // 2
        return wf.at[1, place, pl.ds(pl.multiple_of(side * rows, rows), rows), :]

    def twin_copy():
        i = slot('twin')
        part = half(place_of[2], g)
        return pltpu.make_async_remote_copy(src_ref=part, dst_ref=part, send_sem=send_sem.at[i], recv_sem=recv_sem.at[i], device_id=twin, device_id_type=MESH)

    def twin_arrives():
        i = slot('twin')
        part = half(place_of[2], 1 - g)
        pltpu.make_async_remote_copy(src_ref=part, dst_ref=part, send_sem=send_sem.at[i], recv_sem=recv_sem.at[i], device_id=twin, device_id_type=MESH).wait_recv()

    def relay_half(i, side):
        part = half(place_of[2], side)
        send(('half relay', i), 0, (1,), lambda j: part, part)

    def first_direct(k):
        for a in range(3):
            arrive(('first', k, a), 0, 1, span(k, place_of[1], a))

    def first_relayed(k):
        for a in range(3):
            arrive(('first relay', k, a), 0, 1, span(k, place_of[3], a))
    send_field(0, (2,))
    for a in range(3):
        send_first(0, a, 2)
    for dz in (-1, 1):
        send_field(dz, (0,))
    send_field(0, (1,))
    for a in range(3):
        send_first(0, a, 1)
    load_next = [load(w_first.at[1, a], wf.at[1, c, pl.ds(a * SPAN, TAPS), :]) for a in range(3)]
    load_rest = [load(w_middle, wm.at[0:STEPS])]
    for a in range(3):
        for b in range(3):
            load_rest.append(load(w_last.at[1, a, b], wl_next.at[0, a, :, pl.ds(b * C, C), :]))
    for a in range(3):
        load_rest.append(load(w_last.at[0, a], wl.at[:, :, pl.ds(a * C, C), :]))

    def from_columns(a):
        part = whole.at[a, theirs if a == 2 else pair, :]
        if a == 2:
            arrive('field', 0, 2, part)
            for dz in (-1, 1):
                send('field pass', dz, (0,), lambda j: part, whole.at[2 - dz, theirs, :])
        elif a in (1, 3):
            arrive('field', 2 - a, 0, whole.at[a, mine, :])
            arrive('field pass', 2 - a, 0, whole.at[a, theirs, :])
        tag = ('field relay', a)
        relay = copy(tag, 0, 1, part, part)
        when_side(a - 2, relay.start)
        started.append((a - 2, relay))

    def from_core(a):
        if a == 2:
            arrive('field', 0, 1, whole.at[2, rows_of(place_of[1]), :])
            part = whole.at[2, rows_of(place_of[3]), :]
        else:
            part = whole.at[a, other_pair, :]
        i = slot(('field relay', a), 0, 1)

        def wait():
            pltpu.make_async_remote_copy(src_ref=part, dst_ref=part, send_sem=send_sem.at[i], recv_sem=recv_sem.at[i], device_id=peer(0, 1), device_id_type=MESH).wait_recv()
        when_side(a - 2, wait)
    line = lax.broadcasted_iota(jnp.int32, (C, C), 0)

    def hits(k, channel):
        return (channel == order_in[k:k + 1, :]).astype(F32).T.astype(BF16)
    block = lax.div(line, own)
    perm[0] = hits(0, (2 * lax.rem(block, 2) + lax.div(block, 2)) * own + lax.rem(line, own))
    perm[1] = hits(1, line)
    sent = HALF + lax.div(line, 2 * share) * share + lax.rem(line, share)
    low = lax.rem(lax.div(line, share), 2) == 0
    perm[2] = hits(1, jnp.where(low, sent, -1))
    perm[3] = hits(1, jnp.where(low, -1, sent))
    for k in range(STEPS):
        bias2[k] = jnp.broadcast_to(b2_in[k:k + 1, :].astype(F32), (128, units)).T
        bias3[k] = jnp.broadcast_to(b3_in[k:k + 1, :].astype(F32), (128, C)).T
    y = lax.rem(lax.broadcasted_iota(jnp.int32, (1, NXY), 1), NY)
    lane = lax.broadcasted_iota(jnp.int32, (1, NXY), 1)

    def keep(values, e):
        if e == 0:
            return jnp.where(y == NY - 1, 0.0, values)
        if e == 2:
            return jnp.where(y == 0, 0.0, values)
        return values

    def shifted(b, e):
        start = PAD + NY * (b - 1) + (e - 1)
        return slice(start, start + NXY)

    def wide(column):
        return jnp.concatenate([column.astype(F32)] * (NXY // 128), axis=1)

    def lay(a, front, base=None):
        base = a * SPAN if base is None else base
        for e in range(3):
            xpad[e, a * HALF:(a + 1) * HALF, PAD:PAD + NXY] = keep(front, e).astype(BF16)
        for b in range(3):
            for e in range(3):
                at = base + (b * 3 + e) * HALF
                if not isinstance(at, int):
                    at = pl.multiple_of(at, HALF)
                patches[pl.ds(at, HALF), :] = xpad[e, a * HALF:(a + 1) * HALF, shifted(b, e)]

    def convolve(k, place, p, base=None):
        rows = place * units if isinstance(place, int) else pl.multiple_of(place * units, units)
        one = lax.dot_general(wf[k, place], patches[pl.ds(p * SPAN if base is None else base, 3 * SPAN), :], (((0,), (0,)), ((), ())), preferred_element_type=F32)
        hidden[p, pl.ds(rows, units), :] = jnp.maximum(one, 0.0).astype(BF16)

    def finish():
        for wanted, one in far_started:
            pl.when(wanted)(one.wait_send)
        for dz, one in started:
            when_side(dz, one.wait_send)
    from_columns(2)
    for one in load_next:
        one.wait()
    relay_first(0, 0)
    for a in (1, 3):
        from_columns(a)
    relay_first(0, 1)
    relay_first(0, 2)
    send('half', 0, (2,), lambda j: half(c, g), half(c, g))
    for a in (2, 1, 3):
        from_core(a)
        if a == 2:
            permuted = jnp.dot(perm[0], whole[2], preferred_element_type=F32)
            back[...] = permuted
            front = permuted[:HALF]
        else:
            front = jnp.dot(perm[0, 0:HALF, :], whole[a], preferred_element_type=F32)
        fronts[a] = front.astype(BF16)
        lay(a, front)
    send_far('pair', (0,), (1,), whole.at[2, pair, :], whole.at[0, pair, :])
    convolve(0, c, 1)
    first_direct(0)
    convolve(0, place_of[1], 1)
    convolve(0, place_of[2], 1)
    first_relayed(0)
    convolve(0, place_of[3], 1)
    for one in load_rest:
        one.wait()
    summed = jnp.dot(wm[0], hidden[1], preferred_element_type=F32)
    two = jnp.maximum(summed + wide(bias2[0]), 0.0)
    for e in range(3):
        hpad[e, :, PAD:PAD + NXY] = keep(two, e).astype(BF16)
    for b in range(3):
        for e in range(3):
            at = (b * 3 + e) * units
            patches3[at:at + units, :] = hpad[e, :, shifted(b, e)]
    weights = jnp.concatenate([wl[b, e] for b in range(3) for e in range(3)], axis=1)
    parts = jnp.dot(weights, patches3[...], preferred_element_type=F32)
    for s in range(n_chan):
        for a in range(3):
            at = a * C + s * share
            psend[s, a] = jnp.concatenate([parts[at:at + share], parts[at + HALF:at + HALF + share]], axis=0).astype(BF16)
    for dz in (-1, 1):
        send('parts', dz, (2, 3, 1, 0), lambda j: psend.at[place_of[j], 1 - dz], precv.at[1 - dz, c])
    send('parts', 0, (2, 3, 1), lambda j: psend.at[place_of[j], 1], precv.at[1, c])
    precv[1, c] = psend[c, 1]
    arrive('half', 0, 2, half(place_of[2], g))
    one = twin_copy()
    one.start()
    started.append((0, one))
    relay_half(0, g)
    for a in range(3):
        send_first(1, a, 1)
    send('bias', 0, (1,), lambda j: b2_rows.at[0], b2_rows.at[1])
    send('middle', 0, (1,), lambda j: wm.at[1], wm.at[2])
    send('last', 0, (1,), lambda j: wl_next.at[0], wl_next.at[1])
    for j in (1, 2, 3):
        arrive('parts', 0, j, precv.at[1, place_of[j]])
    total = precv[1, 0].astype(F32)
    for s in range(1, n_chan):
        total = total + precv[1, s].astype(F32)
    for a in (0, 2):
        for j in range(n_chan):
            arrive('parts', 1 - a, j, precv.at[a, place_of[j]])
    for a in (0, 2):
        for s in range(n_chan):
            total = total + precv[a, s].astype(F32)
    scales = pl.ds(pl.multiple_of(c * share, share), share)
    shifts = pl.ds(pl.multiple_of(HALF + c * share, share), share)
    arg = total[:share] + wide(bias3[0, scales, :]) + 2.0
    coupled = (back[shifts, :] + total[share:] + wide(bias3[0, shifts, :])) * jax.nn.sigmoid(arg)
    packed = jnp.concatenate([coupled[:, :NXY // 2], coupled[:, NXY // 2:]], axis=0)
    csend[...] = packed.astype(BF16)
    for dz in (-1, 1):
        send('coupled', dz, (3, 2, 0, 1), lambda j: csend, cgot.at[2 - dz, c])
    send('coupled', 0, (3, 2, 1), lambda j: csend, cgot.at[2, c])
    send_far('coupled', (2, 0), (3, 1), csend, cgot.at[0, c])
    cgot[2, c] = packed.astype(BF16)

    def log_means(k, arg):
        soft = jnp.minimum(arg, 0.0) - jnp.log1p(jnp.exp(-jnp.abs(arg)))
        means = jnp.broadcast_to(jnp.sum(soft, axis=1, keepdims=True) * (1.0 / NXY), (share, share))
        diagonal = lax.broadcasted_iota(jnp.int32, (share, share), 0) == lax.broadcasted_iota(jnp.int32, (share, share), 1)
        logscale[k] = jnp.sum(jnp.where(diagonal, means, 0.0), axis=0, keepdims=True)
    log_means(0, arg)
    far_arrives('pair', 0, whole.at[0, pair, :])
    far_arrives('pair', 1, whole.at[0, other_pair, :])
    front = jnp.dot(perm[0, 0:HALF, :], whole[0], preferred_element_type=F32)
    fronts[0] = front.astype(BF16)
    arrive('bias', 0, 1, b2_rows.at[1])
    bias2[2] = jnp.broadcast_to(b2_rows[1, 0:1, :].astype(F32), (128, units)).T
    arrive('middle', 0, 1, wm.at[2])
    arrive('last', 0, 1, wl_next.at[1])
    first_direct(1)
    arrive(('half relay', 0), 0, 1, half(place_of[3], g))
    twin_arrives()
    relay_half(1, 1 - g)

    def front_of(a, rows):
        kept = jnp.dot(perm[1, 0:rows, 0:HALF], fronts[a], preferred_element_type=F32)
        got = jnp.concatenate([cgot[a, s] for s in range(n_chan)], axis=0)
        halves = [jnp.dot(perm[i, 0:rows, :], got, preferred_element_type=F32) for i in (2, 3)]
        return kept + jnp.concatenate(halves, axis=1)

    def coupled_arrives(a):
        if a == 0:
            for j in (1, 2, 3, 0):
                far_arrives('coupled', j, cgot.at[0, place_of[j]])
            return
        for j in (1, 2, 3, 0):
            if (a, j) != (2, 0):
                arrive('coupled', 2 - a, j, cgot.at[a, place_of[j]])
    for a in (2, 1, 3):
        coupled_arrives(a)
        if a == 2:
            permuted = front_of(2, C)
            back[...] = permuted
            front = permuted[:HALF]
        else:
            front = front_of(a, HALF)
        lay(a, front)
    arrive(('half relay', 1), 0, 1, half(place_of[3], 1 - g))
    for s in range(n_chan):
        convolve(1, s, 1)
    coupled_arrives(0)
    lay(0, front_of(0, HALF), core * 4 * SPAN)
    for s in range(n_chan):
        convolve(1, s, 0, pl.multiple_of(core * 2 * SPAN, 2 * SPAN))

    def keep_two(two, at):
        left = jnp.where(y == 0, 0.0, pltpu.roll(two, 1, 1))
        right = jnp.where(y == NY - 1, 0.0, pltpu.roll(two, NXY - 1, 1))
        for e, values in enumerate((left, two, right)):
            rows = two.shape[0]
            patches3[at + e * rows:at + (e + 1) * rows, :] = values.astype(BF16)
    two = jnp.dot(wm[1], hidden[1], preferred_element_type=F32) + wide(bias2[1])
    keep_two(jnp.maximum(two, 0.0), 0)
    bias = jnp.concatenate([wide(bias2[1]), wide(bias2[2])], axis=0)
    middle = jnp.concatenate([wm[1], wm[2]], axis=0)
    two = jnp.maximum(jnp.dot(middle, hidden[0], preferred_element_type=F32) + bias, 0.0)
    beside = jnp.where(core == 0, z > 0, z < n_slab - 1)
    keep_two(jnp.where(beside, two, 0.0), 3 * units)
    weights = jnp.concatenate([wl_next[0, 1, e] for e in range(3)] + [wl_next[i, 2 * core, e] for e in range(3) for i in range(2)], axis=1)
    parts = jnp.dot(weights, patches3[...], preferred_element_type=F32)
    part = parts[C:2 * C]
    part = part + jnp.where(lane < NY, 0.0, pltpu.roll(parts[0:C], NY, 1))
    part = part + jnp.where(lane >= NXY - NY, 0.0, pltpu.roll(parts[2 * C:], NXY - NY, 1))
    for i in range(2):
        at = i * own
        net_send[i] = jnp.concatenate([part[at:at + own], part[HALF + at:HALF + at + own]], axis=0).astype(BF16)
    for s in range(n_chan):
        rows = part[s * share:(s + 1) * share]
        scale_send[s] = jnp.concatenate([rows[:, :NXY // 2], rows[:, NXY // 2:]], axis=0).astype(BF16)
    nets = []
    for j in (3, 2, 1):
        to = place_of[j]
        one = copy('net', 0, j, net_send.at[lax.rem(to, 2)], net_recv.at[j])
        nets.append((to, one))
        pl.when(to >= n_chan // 2)(one.start)
        send('scale', 0, (j,), lambda j: scale_send.at[place_of[j]], scale_recv.at[j])
    net[...] = part + wide(bias3[1])
    kept = pl.ds(pl.multiple_of(lax.rem(c, 2) * own, own), own)
    moved = pl.ds(pl.multiple_of(HALF + lax.rem(c, 2) * own, own), own)

    @pl.when(c < n_chan // 2)
    def _():
        flowed[...] = back[kept, :]

    @pl.when(c >= n_chan // 2)
    def _():
        scaled, added = (net[kept, :], net[moved, :])
        for j in (1, 2, 3):
            arrive('net', 0, j, net_recv.at[j])
            got = net_recv[j].astype(F32)
            scaled, added = (scaled + got[:own], added + got[own:])
        flowed[...] = (back[moved, :] + added) * jax.nn.sigmoid(scaled + 2.0)
    arg = net[scales, :] + 2.0
    for j in (1, 2, 3):
        arrive('scale', 0, j, scale_recv.at[j])
        got = scale_recv[j].astype(F32)
        arg = arg + jnp.concatenate([got[:share], got[share:]], axis=1)
    log_means(1, arg)
    for to, one in nets:
        pl.when(to >= n_chan // 2)(one.wait_send)
    finish()


def store(moved, means, flowed, logscale):
    flowed[:, 0, :] = moved[...]
    logscale[...] = means[...]


def local(field, order, w_first, b_first, w_middle, b_middle, w_last, b_last):
    n_chan = lax.axis_size('chan')
    share = HALF // n_chan
    own = C // n_chan
    units = w_first.shape[1]
    vmem = pl.BlockSpec(memory_space=pltpu.VMEM)
    hbm = pl.BlockSpec(memory_space=pl.ANY)
    moved, means = pl.pallas_call(kernel, out_shape=(pltpu.VMEM((own, NXY), F32), pltpu.VMEM((STEPS, 1, share), F32)), in_specs=[hbm] * 8, out_specs=(vmem, vmem), scratch_shapes=[pltpu.VMEM((own, NXY), F32), pltpu.VMEM(order.shape, jnp.int32), pltpu.VMEM(b_first.shape, BF16), pltpu.VMEM(b_middle.shape, BF16), pltpu.VMEM(b_last.shape, BF16), pltpu.VMEM((STEPS, n_chan, 3 * SPAN, units), BF16), pltpu.VMEM((STEPS + 1, units, n_chan * units), BF16), pltpu.VMEM((3, 3, 3 * C, units), BF16), pltpu.VMEM((2, 3, 3, 3 * C, units), BF16), pltpu.VMEM((STEPS + 1, units, 128), F32), pltpu.VMEM((STEPS, C, 128), F32), pltpu.VMEM((4, C, C), BF16), pltpu.VMEM((4, C, NXY), BF16), pltpu.VMEM((3, 5 * HALF, NXY + 2 * PAD), BF16), pltpu.VMEM((5 * SPAN, NXY), BF16), pltpu.VMEM((2, n_chan * units, NXY), BF16), pltpu.VMEM((3, units, NXY + 2 * PAD), BF16), pltpu.VMEM((9 * units, NXY), BF16), pltpu.VMEM((n_chan, 3, 2 * share, NXY), BF16), pltpu.VMEM((3, n_chan, 2 * share, NXY), BF16), pltpu.VMEM((C, NXY), F32), pltpu.VMEM((2 * share, NXY // 2), BF16), pltpu.VMEM((4, n_chan, 2 * share, NXY // 2), BF16), pltpu.VMEM((4, HALF, NXY), BF16), pltpu.VMEM((2, 2 * own, NXY), BF16), pltpu.VMEM((n_chan, 2 * own, NXY), BF16), pltpu.VMEM((n_chan, 2 * share, NXY // 2), BF16), pltpu.VMEM((n_chan, 2 * share, NXY // 2), BF16), pltpu.VMEM((C, NXY), F32), pltpu.VMEM((2, 16, units), BF16), pltpu.SemaphoreType.DMA((32,)), pltpu.SemaphoreType.DMA((SEMS,)), pltpu.SemaphoreType.DMA((SEMS,))], compiler_params=pltpu.CompilerParams(collective_id=0, has_side_effects=True, vmem_limit_bytes=62 << 20))(field, order, jnp.swapaxes(w_first, 1, 2).reshape(STEPS, 3, TAPS, units), b_first, w_middle, b_middle, w_last.reshape(STEPS, 3, 3, 3, C, units), b_last)
    moved, means = (pltpu.with_memory_space_constraint(v, pltpu.VMEM) for v in (moved, means))
    flowed, logscale = pl.pallas_call(store, out_shape=(jax.ShapeDtypeStruct(field.shape, F32), jax.ShapeDtypeStruct((STEPS, 1, share), F32)), in_specs=[vmem, vmem], out_specs=(vmem, vmem))(moved, means)
    return (flowed, jnp.swapaxes(logscale, 1, 2))


def solution(mesh):
    return jax.shard_map(local, mesh=mesh, in_specs=(P('chan', ('groups', 'slab'), None), P(), P(None, 'chan', None), P(None, 'chan'), P(None, 'chan', None), P(None, 'chan'), P(None, None, 'chan'), P()), out_specs=(P('chan', ('groups', 'slab'), None), P(None, 'chan', ('groups', 'slab'))), check_vma=False)
```
